128 devices in a mesh: lat: 32 (over y, x, core), lev: 4 (over z).
Axes of the slice: x: 4, y: 4, z: 4, core: 2. Of those that a mesh axis runs over, the one named last changes fastest.
Arguments:
- adjoint_grid: bfloat16 [32, 64, 2, 5136], P('lev', 'lat'), may hold values from -6 to 6
- lower_diffusion: float32 [32, 64, 5136], P(None, 'lat', 'lev'), may hold values from 0.2 to 20
- upper_diffusion: float32 [32, 64, 5136], P(None, 'lat', 'lev'), may hold values from 0.2 to 20
- row_lengths: int32 [32], replicated, may hold values from 1280 to 5136, as said below
- wave_order: int32 [1280], replicated, may hold values from 0 to 1279, each once
Outputs:
- spectral: float32 [1280, 2, 2, 32, 64], P('lat', None, None, 'lev')
The draws below stay inside these ranges and needn't reach their ends.
Inputs may be any that keep to these rules, and one draw needn't show every extreme that they name: `row_lengths`: lengths never fall from pole to equator; the first is 1280 and the last 5136.
All inputs are finite; a program needn't handle non-finite values.
Results may differ from the reference program's by a relative error of at most 0.0037.
Values may be sent and summed in bfloat16 or wider, within the bound.
No kernel may reach another device: no remote copies, remote signals or barrier semaphores. Data moves between devices by JAX's collectives and lax.ppermute only.
A program may use at most 128 MiB of HBM per device.

```python
import math
import jax
import jax.numpy as jnp
from jax import lax

LMAX = 5136
MW = 1280
LEV = 32
FIELDS = 2
NLAT = 64
NH = 32


def draw_row_lengths(key, part):
    values = jax.random.randint(key, (NH,), MW, LMAX + 1)
    ordered = jnp.sort(values)
    return ordered.at[0].set(MW).at[NH - 1].set(LMAX)


def level_of(stream_key, dims, shards, smallest, top_value):
    level = 1.0
    for dim, blocks in shards:
        heights = jax.random.uniform(jax.random.fold_in(jax.random.fold_in(stream_key, 6), dim), (blocks,), jnp.float32, smallest / len(shards), top_value / len(shards))
        level = level * jnp.repeat(jnp.exp(heights), dims[dim] // blocks).reshape((-1,) + (1,) * (len(dims) - 1 - dim))
    return level


def centred(rng, shape, spread, limit, shards=(), kind=jnp.bfloat16):
    level = level_of(rng, shape, shards, -0.22, 0.18) if shards else 1.0
    array = jax.random.normal(rng, shape, jnp.float32) * spread * level
    return jnp.minimum(jnp.maximum(array, -limit), limit).astype(kind)


def setup_inputs(seed: int = 0) -> dict:
    keys = jax.random.split(jax.random.key(seed), 6)
    adjoint_grid = centred(keys[0], (LEV, NLAT, FIELDS, LMAX), 1.0, 6.0, ((0, 4), (1, 32)))
    lower_diffusion = jnp.clip(jnp.exp(math.log(20.0) - 4.6051702 * jax.random.uniform(keys[1], (LEV, NLAT, LMAX), jnp.float32) ** level_of(keys[1], (LEV, NLAT, LMAX), ((1, 32), (2, 4)), -0.2, 0.2)), 0.2, 20.0)
    upper_diffusion = jnp.clip(jnp.exp(math.log(20.0) - 4.6051702 * jax.random.uniform(keys[2], (LEV, NLAT, LMAX), jnp.float32) ** level_of(keys[2], (LEV, NLAT, LMAX), ((1, 32), (2, 4)), -0.2, 0.2)), 0.2, 20.0)
    row_lengths = draw_row_lengths(jax.random.fold_in(keys[5], 71), 0)
    wave_order = jax.random.permutation(keys[4], MW).astype(jnp.int32)
    return {"adjoint_grid": adjoint_grid, "lower_diffusion": lower_diffusion, "upper_diffusion": upper_diffusion, "row_lengths": row_lengths, "wave_order": wave_order}


TWO_PI = 6.283185307179586

def fourier_basis(length, points, offset, wavenumbers):
    points_index = offset + lax.iota(jnp.int32, points)
    wave_index = lax.iota(jnp.int32, wavenumbers)
    product_index = points_index[:, None] * wave_index[None, :] % length
    phase_angle = TWO_PI * product_index.astype(jnp.float32) / length.astype(jnp.float32)
    inside = (points_index[:, None] < length) & (2 * wave_index[None, :] < length)
    cos_part = jnp.where(inside, jnp.cos(phase_angle), 0.0).astype(jnp.bfloat16)
    sin_part = jnp.where(inside, -jnp.sin(phase_angle), 0.0).astype(jnp.bfloat16)
    return jnp.concatenate([cos_part, sin_part], axis=1)

def vertical_adjoint(values_in, lower_diffusion, upper_diffusion):
    levels = values_in.shape[0]
    final_level = levels - 1
    ratios = []
    right_parts = []
    for level in range(levels):
        if level == 0:
            pivot = 1.0 + upper_diffusion[0]
            right_part = values_in[0] / pivot
        else:
            if level == final_level:
                diagonal_term = 1.0 + lower_diffusion[level]
            else:
                diagonal_term = 1.0 + lower_diffusion[level] + upper_diffusion[level]
            pivot = diagonal_term + upper_diffusion[level - 1] * ratios[level - 1]
            right_part = (values_in[level] + upper_diffusion[level - 1] * right_parts[level - 1]) / pivot
        right_parts.append(right_part)
        if level < final_level:
            ratios.append(-lower_diffusion[level + 1] / pivot)
    current = right_parts[final_level]
    results = [current]
    for level in range(final_level - 1, -1, -1):
        current = right_parts[level] - ratios[level] * current
        results.append(current)
    return jnp.stack(results[::-1])

def reference(adjoint_grid, lower_diffusion, upper_diffusion, row_lengths, wave_order):
    solved = vertical_adjoint(adjoint_grid.astype(jnp.float32), lower_diffusion[:, :, None, :], upper_diffusion[:, :, None, :]).astype(jnp.bfloat16)

    def one_pair(pair_index):
        length = row_lengths[pair_index]
        basis = fourier_basis(length, LMAX, 0, MW).astype(jnp.float32)
        northern_rows = lax.dynamic_index_in_dim(solved, pair_index, 1, keepdims=False)
        southern_rows = lax.dynamic_index_in_dim(solved, pair_index + NH, 1, keepdims=False)
        stacked = jnp.stack([northern_rows, southern_rows]).astype(jnp.float32).reshape(2 * LEV * FIELDS, LMAX)
        product = jnp.dot(stacked, basis, precision=lax.Precision.HIGHEST, preferred_element_type=jnp.float32) / jnp.sqrt(length.astype(jnp.float32))
        product = product.reshape(2, LEV, FIELDS, 2, MW)
        return (product[0] + product[1], product[0] - product[1])
    symmetric, antisymmetric = lax.map(one_pair, jnp.arange(NH, dtype=jnp.int32))
    paired = jnp.concatenate([symmetric, antisymmetric], axis=0)
    ordered = jnp.take(paired, wave_order, axis=4)
    return jnp.transpose(ordered, (4, 3, 2, 1, 0))
```

```python
import jax
import jax.numpy as jnp
from jax import lax
from jax.experimental import pallas as pl
from jax.experimental.pallas import tpu as pltpu
from jax.sharding import PartitionSpec as P

LANE = 128
DEEP = 256
TWO_PI = 6.283185307179586
VMEM = pl.BlockSpec(memory_space=pltpu.VMEM)
SMEM = pl.BlockSpec(memory_space=pltpu.SMEM)


def sizes(points, lev_count):
    block = points // lev_count
    step = block // LANE * LANE
    window = step + LANE
    return block, step, window


def pack_kernel(lev_count, points, x_ref, *outs):
    block, step, window = sizes(points, lev_count)
    levels, rows, fields = x_ref.shape[:3]
    last = points - lev_count * step
    me = lax.axis_index("lev")
    for shift, out in enumerate(outs):
        to = lax.rem(me + shift, lev_count)
        base = pl.multiple_of(to * step, LANE)
        for row in range(rows):
            for level in range(levels):
                low = fields * level
                out[row, low : low + fields, :step] = x_ref[level, row, :, pl.ds(base, step)]

        @pl.when(to < lev_count - 1)
        def _():
            tail = pl.multiple_of(to * step + step, LANE)
            for row in range(rows):
                for level in range(levels):
                    low = fields * level
                    out[row, low : low + fields, step:] = x_ref[level, row, :, pl.ds(tail, LANE)]

        @pl.when(to == lev_count - 1)
        def _():
            for row in range(rows):
                for level in range(levels):
                    low = fields * level
                    out[row, low : low + fields, step : step + last] = x_ref[level, row, :, lev_count * step :]


def turn(multiple, length):
    inverse = 1.0 / length
    rest = multiple - jnp.floor(multiple * inverse) * length
    rest = jnp.where(rest < 0.0, rest + length, rest)
    rest = jnp.where(rest >= length, rest - length, rest)
    quarter = jnp.floor(4.0 * rest * inverse + 0.5)
    angle = (4.0 * rest - quarter * length) * ((TWO_PI / 4.0) * inverse)
    square = angle * angle
    sine = angle + angle * square * (-1.6666654611e-1 + square * (8.3321608736e-3 + square * -1.9515295891e-4))
    cosine = 1.0 - 0.5 * square + square * square * (
        4.166664568298827e-2 + square * (-1.388731625493765e-3 + square * 2.443315711809948e-5)
    )
    odd = (quarter == 1.0) | (quarter == 3.0)
    real = jnp.where(odd, sine, cosine)
    imag = jnp.where(odd, cosine, sine)
    real = jnp.where((quarter == 1.0) | (quarter == 2.0), -real, real)
    imag = jnp.where((quarter == 2.0) | (quarter == 3.0), imag, -imag)
    return real, imag


def prepare_kernel(
    lev_count, points, lengths_ref, wave_ref, lower_ref, upper_ref, fine_ref, coarse_ref, first_ref, second_ref, third_ref
):
    block, step, window = sizes(points, lev_count)
    rows = fine_ref.shape[0]
    waves = wave_ref.shape[1]
    halves = lengths_ref.shape[0]
    wave = wave_ref[...].astype(jnp.float32)
    me_lat = lax.axis_index("lat")
    me_lev = lax.axis_index("lev")
    coarse_rows = coarse_ref.shape[2]
    small = lax.broadcasted_iota(jnp.int32, (16, 1), 0).astype(jnp.float32)
    blocks = lax.broadcasted_iota(jnp.int32, (coarse_rows, 1), 0).astype(jnp.float32)
    for row in range(rows):
        whole = lengths_ref[lax.rem(me_lat * rows + row, halves)]
        length = jnp.full((1, 1), whole, jnp.int32).astype(jnp.float32)
        near_real, near_imag = turn(wave * small, length)
        far_real, far_imag = turn(wave * (16.0 * small), length)
        for part in range(16):
            one_real = far_real[part : part + 1]
            one_imag = far_imag[part : part + 1]
            low = 16 * part
            fine_ref[row, low : low + 16, :waves] = (near_real * one_real - near_imag * one_imag).astype(jnp.bfloat16)
            fine_ref[row, low : low + 16, waves:] = (near_real * one_imag + near_imag * one_real).astype(jnp.bfloat16)
        real, imag = turn(wave * (float(DEEP) * blocks), length)
        scale = jnp.where(2.0 * wave < length, 1.0 / jnp.sqrt(length), 0.0)
        coarse_ref[row, 0] = real * scale
        coarse_ref[row, 1] = imag * scale

    levels = lower_ref.shape[0]
    own = first_ref.shape[2] // 2
    ratio = None
    for level in range(levels):
        upper = upper_ref[level]
        if level == 0:
            pivot = 1.0 + upper
            above = jnp.zeros_like(upper)
        else:
            diagonal = 1.0 + lower_ref[level]
            if level < levels - 1:
                diagonal = diagonal + upper
            above = upper_ref[level - 1]
            pivot = diagonal + above * ratio
        inverse = 1.0 / pivot
        if level < levels - 1:
            ratio = -lower_ref[level + 1] * inverse
        else:
            ratio = jnp.zeros_like(inverse)
        chunk, inner = divmod(level, own)
        for out, value in ((first_ref, inverse), (second_ref, above * inverse), (third_ref, ratio)):
            for row in range(rows):
                out[chunk, row, 2 * inner : 2 * inner + 2, :block] = jnp.broadcast_to(value[row : row + 1], (2, block))
    for out in (first_ref, second_ref, third_ref):
        for chunk in range(out.shape[0]):
            for row in range(rows):
                out[chunk, row] = pltpu.roll(out[chunk, row], me_lev * (block - step), 1)


def solve_kernel(lev_count, points, lengths_ref, first_ref, second_ref, third_ref, *refs):
    block, step, window = sizes(points, lev_count)
    sources, outs, work = refs[:lev_count], refs[lev_count : 2 * lev_count], refs[-1]
    rows = work.shape[1]
    own = work.shape[2] // 2
    levels = lev_count * own
    halves = lengths_ref.shape[0]
    me_lat = lax.axis_index("lat")
    me_lev = lax.axis_index("lev")
    for shift, source in enumerate(sources):
        chunk = lax.rem(me_lev + lev_count - shift, lev_count)
        for row in range(rows):
            work[chunk, row] = source[row].astype(jnp.float32)
    lane = lax.broadcasted_iota(jnp.int32, (1, window), 1)
    offset = me_lev * (block - step)
    inside = []
    for row in range(rows):
        whole = lengths_ref[lax.rem(me_lat * rows + row, halves)]
        inside.append((lane >= offset) & (lane < offset + block) & (lane + me_lev * step < whole))
    for row in range(rows):
        part = None
        for level in range(levels):
            chunk, inner = divmod(level, own)
            at = (chunk, row, slice(2 * inner, 2 * inner + 2))
            value = work[at] * first_ref[at]
            part = value if part is None else value + second_ref[at] * part
            work[at] = part
        current = None
        for level in range(levels - 1, -1, -1):
            chunk, inner = divmod(level, own)
            at = (chunk, row, slice(2 * inner, 2 * inner + 2))
            current = work[at] if current is None else work[at] - third_ref[at] * current
            work[at] = current
    for shift, out in enumerate(outs):
        chunk = lax.rem(me_lev + shift, lev_count)
        for row in range(rows):
            out[row] = jnp.where(inside[row], work[chunk, row], 0.0).astype(jnp.bfloat16)


def fourier_kernel(lev_count, points, fine_ref, coarse_ref, *refs):
    block, step, window = sizes(points, lev_count)
    sources, out_ref, spectra, turned = refs[:lev_count], refs[-3], refs[-2], refs[-1]
    rows = fine_ref.shape[0]
    waves = fine_ref.shape[2] // 2
    per = step // DEEP
    me_lev = lax.axis_index("lev")
    members = sources[0].shape[1]
    for row in range(rows):
        main = jnp.concatenate(
            [source[row, :, DEEP * a : DEEP * (a + 1)] for source in sources for a in range(per)], axis=0
        )
        tail = jnp.concatenate([source[row, :, step:] for source in sources], axis=0)
        for tile in range(waves // DEEP):
            low = DEEP * tile
            cos_table = fine_ref[row, :, low : low + DEEP]
            sin_table = fine_ref[row, :, waves + low : waves + low + DEEP]
            main_cos = jnp.dot(main, cos_table, preferred_element_type=jnp.float32)
            main_sin = jnp.dot(main, sin_table, preferred_element_type=jnp.float32)
            tail_cos = jnp.dot(tail, cos_table[:LANE], preferred_element_type=jnp.float32)
            tail_sin = jnp.dot(tail, sin_table[:LANE], preferred_element_type=jnp.float32)
            real = jnp.zeros((members, DEEP), jnp.float32)
            imag = jnp.zeros((members, DEEP), jnp.float32)
            for shift in range(lev_count):
                begin = per * lax.rem(me_lev + lev_count - shift, lev_count)
                for a in range(per + 1):
                    if a < per:
                        pos = members * (per * shift + a)
                        y_cos, y_sin = main_cos[pos : pos + members], main_sin[pos : pos + members]
                    else:
                        pos = members * shift
                        y_cos, y_sin = tail_cos[pos : pos + members], tail_sin[pos : pos + members]
                    c = coarse_ref[row, 0, pl.ds(begin + a, 1), low : low + DEEP]
                    s = coarse_ref[row, 1, pl.ds(begin + a, 1), low : low + DEEP]
                    real = real + (y_cos * c - y_sin * s)
                    imag = imag + (y_sin * c + y_cos * s)
            for half in range(DEEP // LANE):
                at = tile * (DEEP // LANE) + half
                spectra[row, 0, at] = real[:, LANE * half : LANE * (half + 1)]
                spectra[row, 1, at] = imag[:, LANE * half : LANE * (half + 1)]
    for tile in range(waves // LANE):
        low = LANE * tile
        pieces = []
        for row in range(rows):
            one = [
                spectra[row, c, tile, pl.ds(field, members // 2, stride=2), :] for c in range(2) for field in range(2)
            ]
            pieces += one + one
        turned[low : low + LANE, :] = jnp.concatenate(pieces, axis=0).T
    turned[waves:, :] = jnp.zeros((turned.shape[0] - waves, LANE), jnp.float32)
    parts = out_ref.shape[0]
    high = out_ref.shape[1]
    slots = waves // parts
    lane = lax.broadcasted_iota(jnp.int32, (high, LANE), 1)
    left = lax.rem(lane, LANE // 2) < LANE // 4
    for part in range(parts):
        top = turned[slots * part : slots * part + high, :]
        low = turned[slots * part + high : slots * part + 2 * high, :]
        out_ref[part] = jnp.where(left, top, low).astype(jnp.bfloat16)


def pair_kernel(in_ref, out_ref, work):
    parts, high = in_ref.shape[:2]
    slots = out_ref.shape[0]
    grid_rows = out_ref.shape[4]
    rows = grid_rows // parts
    for part in range(parts):
        work[high * part : high * (part + 1), :] = in_ref[part].astype(jnp.float32)
    source = lax.broadcasted_iota(jnp.int32, (parts, grid_rows), 0)
    target = lax.broadcasted_iota(jnp.int32, (parts, grid_rows), 1)
    half = grid_rows // 2
    mixes = []
    for row in range(rows):
        place = rows * source + row
        same = lax.rem(place, half) == lax.rem(target, half)
        sign = jnp.where((target >= half) & (place >= half), -1.0, 1.0)
        mixes.append(jnp.where(same, sign, 0.0).astype(jnp.bfloat16))
    half_lanes = LANE // 2
    for slot in range(high):
        block = work[pl.ds(slot, parts, stride=high), :].T.astype(jnp.bfloat16)
        result = jnp.dot(block[:half_lanes], mixes[0], preferred_element_type=jnp.float32)
        result = result + jnp.dot(block[half_lanes:], mixes[1], preferred_element_type=jnp.float32)
        quarter = half_lanes // 2
        out_ref[slot] = result[:quarter].reshape(out_ref.shape[1:])
        if high + slot < slots:
            out_ref[high + slot] = result[quarter:].reshape(out_ref.shape[1:])


def shift_all(blocks, axis):
    count = lax.axis_size(axis)
    moved = [blocks[0]]
    for shift in range(1, count):
        moved.append(lax.ppermute(blocks[shift], axis, [(i, (i + shift) % count) for i in range(count)]))
    return moved


def body(adjoint_grid, lower_diffusion, upper_diffusion, row_lengths, wave_order):
    lev_count = lax.axis_size("lev")
    lat_count = lax.axis_size("lat")
    levels, rows, fields, points = adjoint_grid.shape
    waves = wave_order.shape[0]
    block, step, window = sizes(points, lev_count)
    f32, bf16 = jnp.float32, jnp.bfloat16
    members = levels * fields
    shape = jax.ShapeDtypeStruct
    packed = pl.pallas_call(
        lambda *refs: pack_kernel(lev_count, points, *refs),
        out_shape=[shape((rows, members, window), bf16)] * lev_count,
        in_specs=[VMEM],
        out_specs=[VMEM] * lev_count,
        name="pack",
    )(adjoint_grid)
    factor = shape((lev_count, rows, members, window), f32)
    fine, coarse, first, second, third = pl.pallas_call(
        lambda *refs: prepare_kernel(lev_count, points, *refs),
        out_shape=[shape((rows, DEEP, 2 * waves), bf16), shape((rows, 2, 24, waves), f32), factor, factor, factor],
        in_specs=[SMEM, VMEM, VMEM, VMEM],
        out_specs=[VMEM] * 5,
        name="prepare",
        cost_estimate=pl.CostEstimate(flops=20_000_000, bytes_accessed=4_000_000, transcendentals=0),
    )(row_lengths, wave_order[None, :], lower_diffusion, upper_diffusion)
    arrived = shift_all(packed, "lev")
    solved = pl.pallas_call(
        lambda *refs: solve_kernel(lev_count, points, *refs),
        out_shape=[shape((rows, members, window), bf16)] * lev_count,
        in_specs=[SMEM] + [VMEM] * (3 + lev_count),
        out_specs=[VMEM] * lev_count,
        scratch_shapes=[pltpu.VMEM((lev_count, rows, members, window), f32)],
        name="solve",
    )(row_lengths, first, second, third, *arrived)
    returned = shift_all(solved, "lev")
    slots = waves // lat_count
    high = 24
    sent = pl.pallas_call(
        lambda *refs: fourier_kernel(lev_count, points, *refs),
        out_shape=shape((lat_count, high, LANE), bf16),
        in_specs=[VMEM] * (2 + lev_count),
        out_specs=VMEM,
        scratch_shapes=[pltpu.VMEM((rows, 2, waves // LANE, members, LANE), f32), pltpu.VMEM((waves + 16, LANE), f32)],
        name="fourier",
    )(fine, coarse, *returned)
    received = lax.all_to_all(sent, "lat", split_axis=0, concat_axis=0, tiled=True)
    return pl.pallas_call(
        pair_kernel,
        out_shape=shape((slots, 2, fields, levels, rows * lat_count), f32),
        in_specs=[VMEM],
        out_specs=VMEM,
        scratch_shapes=[pltpu.VMEM((lat_count * high, LANE), f32)],
        name="pair",
    )(received)


def solution(mesh):
    in_specs = (P("lev", "lat", None, None), P(None, "lat", "lev"), P(None, "lat", "lev"), P(), P())
    out_specs = P("lat", None, None, "lev", None)
    return jax.shard_map(body, mesh=mesh, in_specs=in_specs, out_specs=out_specs, check_vma=False)
```

```python
import jax
import jax.numpy as jnp
from jax import lax
from jax.experimental import pallas as pl
from jax.experimental.pallas import tpu as pltpu
from jax.sharding import PartitionSpec as P

LANE = 128
DEEP = 256
LIMIT = pltpu.CompilerParams(vmem_limit_bytes=24 << 20)
TWO_PI = 6.283185307179586
VMEM = pl.BlockSpec(memory_space=pltpu.VMEM)
ANY = pl.BlockSpec(memory_space=pl.ANY)


def sizes(points, lev_count):
    block = points // lev_count
    step = block // LANE * LANE
    window = step + LANE
    return block, step, window


def pack_kernel(lev_count, shifts, x_hbm, lower_hbm, upper_hbm, lengths_hbm, *refs):
    outs, (lower_ref, upper_ref, limit_ref, x_ref, lengths_ref, sems) = refs[: len(shifts)], refs[len(shifts) :]
    levels, rows, fields, points = x_ref.shape
    _, step, _ = sizes(points, lev_count)
    last = points - lev_count * step
    me = lax.axis_index("lev")
    copies = [
        pltpu.make_async_copy(source, target, sems.at[i])
        for i, (source, target) in enumerate(
            [(x_hbm, x_ref), (lengths_hbm, lengths_ref), (lower_hbm, lower_ref), (upper_hbm, upper_ref)]
        )
    ]
    for copy in copies:
        copy.start()
    copies[0].wait()
    for shift, out in zip(shifts, outs):
        to = lax.rem(me + shift, lev_count)
        base = pl.multiple_of(to * step, LANE)
        for row in range(rows):
            for level in range(levels):
                low = fields * level
                out[row, low : low + fields, :step] = x_ref[level, row, :, pl.ds(base, step)]

        @pl.when(to < lev_count - 1)
        def _():
            tail = pl.multiple_of(to * step + step, LANE)
            for row in range(rows):
                for level in range(levels):
                    low = fields * level
                    out[row, low : low + fields, step:] = x_ref[level, row, :, pl.ds(tail, LANE)]

        @pl.when(to == lev_count - 1)
        def _():
            for row in range(rows):
                for level in range(levels):
                    low = fields * level
                    out[row, low : low + fields, step : step + last] = x_ref[level, row, :, lev_count * step :]

    copies[1].wait()
    first = rows * lax.axis_index("lat")
    for row in range(rows):
        whole = lengths_ref[lax.rem(first + row, lengths_ref.shape[0])]
        limit_ref[row : row + 1, :] = jnp.full((1, LANE), whole, jnp.int32)
    copies[2].wait()
    copies[3].wait()


def turn(multiple, length):
    inverse = 1.0 / length
    rest = multiple - jnp.floor(multiple * inverse) * length
    rest = jnp.where(rest < 0.0, rest + length, rest)
    rest = jnp.where(rest >= length, rest - length, rest)
    quarter = jnp.floor(4.0 * rest * inverse + 0.5)
    angle = (4.0 * rest - quarter * length) * ((TWO_PI / 4.0) * inverse)
    square = angle * angle
    sine = angle + angle * square * (-1.6666654611e-1 + square * (8.3321608736e-3 + square * -1.9515295891e-4))
    cosine = 1.0 - 0.5 * square + square * square * (
        4.166664568298827e-2 + square * (-1.388731625493765e-3 + square * 2.443315711809948e-5)
    )
    odd = (quarter == 1.0) | (quarter == 3.0)
    real = jnp.where(odd, sine, cosine)
    imag = jnp.where(odd, cosine, sine)
    real = jnp.where((quarter == 1.0) | (quarter == 2.0), -real, real)
    imag = jnp.where((quarter == 2.0) | (quarter == 3.0), imag, -imag)
    return real, imag


def table_kernel(limit_ref, wave_ref, after_ref, fine_ref, coarse_ref):
    rows = fine_ref.shape[0]
    waves = wave_ref.shape[1]
    wave = wave_ref[...].astype(jnp.float32)
    coarse_rows = coarse_ref.shape[2]
    small = lax.broadcasted_iota(jnp.int32, (16, 1), 0).astype(jnp.float32)
    blocks = lax.broadcasted_iota(jnp.int32, (coarse_rows, 1), 0).astype(jnp.float32)
    for row in range(rows):
        length = limit_ref[row : row + 1, :1].astype(jnp.float32)
        near_real, near_imag = turn(wave * small, length)
        far_real, far_imag = turn(wave * (16.0 * small), length)
        for part in range(16):
            one_real = far_real[part : part + 1]
            one_imag = far_imag[part : part + 1]
            low = 16 * part
            fine_ref[row, low : low + 16, :waves] = (near_real * one_real - near_imag * one_imag).astype(jnp.bfloat16)
            fine_ref[row, low : low + 16, waves:] = (near_real * one_imag + near_imag * one_real).astype(jnp.bfloat16)
        real, imag = turn(wave * (float(DEEP) * blocks), length)
        scale = jnp.where(2.0 * wave < length, 1.0 / jnp.sqrt(length), 0.0)
        coarse_ref[row, 0] = real * scale
        coarse_ref[row, 1] = imag * scale


def factor_kernel(lev_count, points, lower_ref, upper_ref, after_ref, first_ref, second_ref, third_ref):
    block, step, _ = sizes(points, lev_count)
    rows = first_ref.shape[1]
    me_lev = lax.axis_index("lev")
    levels = lower_ref.shape[0]
    own = first_ref.shape[2] // 2
    ratio = None
    for level in range(levels):
        upper = upper_ref[level]
        if level == 0:
            pivot = 1.0 + upper
            above = jnp.zeros_like(upper)
        else:
            diagonal = 1.0 + lower_ref[level]
            if level < levels - 1:
                diagonal = diagonal + upper
            above = upper_ref[level - 1]
            pivot = diagonal + above * ratio
        inverse = 1.0 / pivot
        if level < levels - 1:
            ratio = -lower_ref[level + 1] * inverse
        else:
            ratio = jnp.zeros_like(inverse)
        chunk, inner = divmod(level, own)
        for out, value in ((first_ref, inverse), (second_ref, above * inverse), (third_ref, ratio)):
            for row in range(rows):
                out[chunk, row, 2 * inner : 2 * inner + 2, :block] = jnp.broadcast_to(value[row : row + 1], (2, block))
    for out in (first_ref, second_ref, third_ref):
        for chunk in range(out.shape[0]):
            for row in range(rows):
                out[chunk, row] = pltpu.roll(out[chunk, row], me_lev * (block - step), 1)


def solve_kernel(lev_count, points, limit_ref, first_ref, second_ref, third_ref, *refs):
    block, step, window = sizes(points, lev_count)
    sources, outs, work = refs[:lev_count], refs[lev_count : 2 * lev_count], refs[-1]
    rows = work.shape[1]
    own = work.shape[2] // 2
    levels = lev_count * own
    me_lev = lax.axis_index("lev")
    for shift, source in enumerate(sources):
        chunk = lax.rem(me_lev + lev_count - shift, lev_count)
        for row in range(rows):
            work[chunk, row] = source[row].astype(jnp.float32)
    lane = lax.broadcasted_iota(jnp.int32, (1, window), 1)
    offset = me_lev * (block - step)
    inside = []
    for row in range(rows):
        whole = limit_ref[row : row + 1, :1]
        inside.append((lane >= offset) & (lane < offset + block) & (lane + me_lev * step < whole))
    for row in range(rows):
        part = None
        for level in range(levels):
            chunk, inner = divmod(level, own)
            at = (chunk, row, slice(2 * inner, 2 * inner + 2))
            value = work[at] * first_ref[at]
            part = value if part is None else value + second_ref[at] * part
            work[at] = part
        current = None
        for level in range(levels - 1, -1, -1):
            chunk, inner = divmod(level, own)
            at = (chunk, row, slice(2 * inner, 2 * inner + 2))
            current = work[at] if current is None else work[at] - third_ref[at] * current
            work[at] = current
    for shift, out in enumerate(outs):
        chunk = lax.rem(me_lev + shift, lev_count)
        for row in range(rows):
            out[row] = jnp.where(inside[row], work[chunk, row], 0.0).astype(jnp.bfloat16)


def fourier_kernel(lev_count, points, fine_ref, coarse_ref, *refs):
    _, step, _ = sizes(points, lev_count)
    sources, out_ref, spectra, turned = refs[:lev_count], refs[-3], refs[-2], refs[-1]
    rows = fine_ref.shape[0]
    waves = fine_ref.shape[2] // 2
    per = step // DEEP
    me_lev = lax.axis_index("lev")
    members = sources[0].shape[1]
    for row in range(rows):
        main = jnp.concatenate(
            [source[row, :, DEEP * a : DEEP * (a + 1)] for source in sources for a in range(per)], axis=0
        )
        tail = jnp.concatenate([source[row, :, step:] for source in sources], axis=0)
        for tile in range(waves // DEEP):
            low = DEEP * tile
            cos_table = fine_ref[row, :, low : low + DEEP]
            sin_table = fine_ref[row, :, waves + low : waves + low + DEEP]
            main_cos = jnp.dot(main, cos_table, preferred_element_type=jnp.float32)
            main_sin = jnp.dot(main, sin_table, preferred_element_type=jnp.float32)
            tail_cos = jnp.dot(tail, cos_table[:LANE], preferred_element_type=jnp.float32)
            tail_sin = jnp.dot(tail, sin_table[:LANE], preferred_element_type=jnp.float32)
            real = jnp.zeros((members, DEEP), jnp.float32)
            imag = jnp.zeros((members, DEEP), jnp.float32)
            for shift in range(lev_count):
                begin = per * lax.rem(me_lev + lev_count - shift, lev_count)
                for a in range(per + 1):
                    if a < per:
                        pos = members * (per * shift + a)
                        y_cos, y_sin = main_cos[pos : pos + members], main_sin[pos : pos + members]
                    else:
                        pos = members * shift
                        y_cos, y_sin = tail_cos[pos : pos + members], tail_sin[pos : pos + members]
                    c = coarse_ref[row, 0, pl.ds(begin + a, 1), low : low + DEEP]
                    s = coarse_ref[row, 1, pl.ds(begin + a, 1), low : low + DEEP]
                    real = real + (y_cos * c - y_sin * s)
                    imag = imag + (y_sin * c + y_cos * s)
            for half in range(DEEP // LANE):
                at = tile * (DEEP // LANE) + half
                spectra[row, 0, at] = real[:, LANE * half : LANE * (half + 1)]
                spectra[row, 1, at] = imag[:, LANE * half : LANE * (half + 1)]
    for tile in range(waves // LANE):
        low = LANE * tile
        pieces = []
        for row in range(rows):
            one = [
                spectra[row, c, tile, pl.ds(field, members // 2, stride=2), :] for c in range(2) for field in range(2)
            ]
            pieces += one + one
        turned[low : low + LANE, :] = jnp.concatenate(pieces, axis=0).T
    turned[waves:, :] = jnp.zeros((turned.shape[0] - waves, LANE), jnp.float32)
    parts = out_ref.shape[0]
    high = out_ref.shape[1]
    slots = waves // parts
    lane = lax.broadcasted_iota(jnp.int32, (high, LANE), 1)
    left = lax.rem(lane, LANE // 2) < LANE // 4
    for part in range(parts):
        top = turned[slots * part : slots * part + high, :]
        low = turned[slots * part + high : slots * part + 2 * high, :]
        out_ref[part] = jnp.where(left, top, low).astype(jnp.bfloat16)


def pair_kernel(in_ref, out_ref, work):
    parts, high = in_ref.shape[:2]
    slots = out_ref.shape[0]
    grid_rows = out_ref.shape[4]
    rows = grid_rows // parts
    for part in range(parts):
        work[high * part : high * (part + 1), :] = in_ref[part].astype(jnp.float32)
    source = lax.broadcasted_iota(jnp.int32, (parts, grid_rows), 0)
    target = lax.broadcasted_iota(jnp.int32, (parts, grid_rows), 1)
    half = grid_rows // 2
    mixes = []
    for row in range(rows):
        place = rows * source + row
        same = lax.rem(place, half) == lax.rem(target, half)
        sign = jnp.where((target >= half) & (place >= half), -1.0, 1.0)
        mixes.append(jnp.where(same, sign, 0.0).astype(jnp.bfloat16))
    half_lanes = LANE // 2
    for slot in range(high):
        block = work[pl.ds(slot, parts, stride=high), :].T.astype(jnp.bfloat16)
        result = jnp.dot(block[:half_lanes], mixes[0], preferred_element_type=jnp.float32)
        result = result + jnp.dot(block[half_lanes:], mixes[1], preferred_element_type=jnp.float32)
        quarter = half_lanes // 2
        out_ref[slot] = result[:quarter].reshape(out_ref.shape[1:])
        if high + slot < slots:
            out_ref[high + slot] = result[quarter:].reshape(out_ref.shape[1:])


def near(x):
    return pltpu.with_memory_space_constraint(x, pltpu.VMEM)


def far(x):
    return pltpu.with_memory_space_constraint(x, pltpu.HBM)


def exchange(blocks, order):
    count = lax.axis_size("lev")
    moved = {0: blocks[0]}
    for shift in order[:-1]:
        moved[shift] = lax.ppermute(blocks[shift], "lev", [(i, (i + shift) % count) for i in range(count)])
    return moved


def body(adjoint_grid, lower_diffusion, upper_diffusion, row_lengths, wave_order):
    lev_count = lax.axis_size("lev")
    lat_count = lax.axis_size("lat")
    levels, rows, fields, points = adjoint_grid.shape
    waves = wave_order.shape[0]
    _, _, window = sizes(points, lev_count)
    f32, bf16 = jnp.float32, jnp.bfloat16
    members = levels * fields
    order = sorted(range(lev_count), key=lambda shift: -min(shift, lev_count - shift))
    windows = pltpu.VMEM((rows, members, window), bf16)
    made = pl.pallas_call(
        lambda *refs: pack_kernel(lev_count, order, *refs),
        out_shape=[windows] * lev_count
        + [pltpu.VMEM(lower_diffusion.shape, f32)] * 2
        + [pltpu.VMEM((rows, LANE), jnp.int32)],
        in_specs=[ANY] * 4,
        out_specs=[VMEM] * (lev_count + 3),
        scratch_shapes=[
            pltpu.VMEM(adjoint_grid.shape, bf16),
            pltpu.SMEM(row_lengths.shape, jnp.int32),
            pltpu.SemaphoreType.DMA((4,)),
        ],
        name="pack",
        compiler_params=LIMIT,
    )(*[far(x) for x in (adjoint_grid, lower_diffusion, upper_diffusion, row_lengths)])
    packed = dict(zip(order, made))
    lower, upper, limit = made[lev_count:]
    arrived = exchange(packed, order)
    factor = pltpu.VMEM((lev_count, rows, members, window), f32)
    factors = pl.pallas_call(
        lambda *refs: factor_kernel(lev_count, points, *refs),
        out_shape=[factor] * 3,
        in_specs=[VMEM, VMEM, ANY],
        out_specs=[VMEM] * 3,
        name="factor",
        compiler_params=LIMIT,
        cost_estimate=pl.CostEstimate(flops=10_000_000, bytes_accessed=4_000_000, transcendentals=0),
    )(near(lower), near(upper), packed[0])
    solved = pl.pallas_call(
        lambda *refs: solve_kernel(lev_count, points, *refs),
        out_shape=[windows] * lev_count,
        in_specs=[VMEM] * (4 + lev_count),
        out_specs=[VMEM] * lev_count,
        scratch_shapes=[pltpu.VMEM((lev_count, rows, members, window), f32)],
        name="solve",
        compiler_params=LIMIT,
    )(near(limit), *[near(x) for x in factors], *[near(arrived[shift]) for shift in range(lev_count)])
    returned = exchange(solved, order)
    fine, coarse = pl.pallas_call(
        table_kernel,
        out_shape=[pltpu.VMEM((rows, DEEP, 2 * waves), bf16), pltpu.VMEM((rows, 2, 24, waves), f32)],
        in_specs=[VMEM, VMEM, ANY],
        out_specs=[VMEM] * 2,
        name="table",
        compiler_params=LIMIT,
        cost_estimate=pl.CostEstimate(flops=10_000_000, bytes_accessed=4_000_000, transcendentals=0),
    )(near(limit), wave_order[None, :], solved[0])
    slots = waves // lat_count
    high = 24
    sent = pl.pallas_call(
        lambda *refs: fourier_kernel(lev_count, points, *refs),
        out_shape=pltpu.VMEM((lat_count, high, LANE), bf16),
        in_specs=[VMEM] * (2 + lev_count),
        out_specs=VMEM,
        scratch_shapes=[
            pltpu.VMEM((rows, 2, waves // LANE, members, LANE), f32),
            pltpu.VMEM((waves + 16, LANE), f32),
        ],
        name="fourier",
        compiler_params=LIMIT,
    )(near(fine), near(coarse), *[near(returned[shift]) for shift in range(lev_count)])
    received = lax.all_to_all(sent, "lat", split_axis=0, concat_axis=0, tiled=True)
    return pl.pallas_call(
        pair_kernel,
        out_shape=jax.ShapeDtypeStruct((slots, 2, fields, levels, rows * lat_count), f32),
        in_specs=[VMEM],
        out_specs=VMEM,
        scratch_shapes=[pltpu.VMEM((lat_count * high, LANE), f32)],
        name="pair",
        compiler_params=LIMIT,
    )(near(received))


def solution(mesh):
    in_specs = (P("lev", "lat", None, None), P(None, "lat", "lev"), P(None, "lat", "lev"), P(), P())
    out_specs = P("lat", None, None, "lev", None)
    return jax.shard_map(body, mesh=mesh, in_specs=in_specs, out_specs=out_specs, check_vma=False)
```

```python
import jax
import jax.numpy as jnp
from jax import lax
from jax.experimental import pallas as pl
from jax.experimental.pallas import tpu as pltpu
from jax.sharding import PartitionSpec as P

LANE = 128
DEEP = 256
LIMIT = pltpu.CompilerParams(vmem_limit_bytes=24 << 20)
TWO_PI = 6.283185307179586
VMEM = pl.BlockSpec(memory_space=pltpu.VMEM)
ANY = pl.BlockSpec(memory_space=pl.ANY)


def sizes(points, lev_count):
    block = points // lev_count
    step = block // LANE * LANE
    window = step + LANE
    return block, step, window


def pack_kernel(lev_count, shifts, x_hbm, lengths_hbm, *refs):
    outs, (limit_ref, x_ref, lengths_ref, sems) = refs[: len(shifts)], refs[len(shifts) :]
    levels, rows, fields, points = x_ref.shape
    _, step, _ = sizes(points, lev_count)
    last = points - lev_count * step
    me = lax.axis_index("lev")
    pairs = [(x_hbm.at[level], x_ref.at[level]) for level in range(levels)]
    pairs += [(lengths_hbm, lengths_ref)]
    copies = [pltpu.make_async_copy(source, target, sems.at[i]) for i, (source, target) in enumerate(pairs)]
    for copy in copies:
        copy.start()
    pieces = len(copies) - 1
    for piece in range(pieces):
        copies[piece].wait()
        some = range(levels * piece // pieces, levels * (piece + 1) // pieces)
        for shift, out in zip(shifts, outs):
            to = lax.rem(me + shift, lev_count)
            base = pl.multiple_of(to * step, LANE)
            for level in some:
                for row in range(rows):
                    low = fields * (rows * level + row)
                    out[low : low + fields, :step] = x_ref[level, row, :, pl.ds(base, step)]
    for shift, out in zip(shifts, outs):
        to = lax.rem(me + shift, lev_count)

        @pl.when(to < lev_count - 1)
        def _():
            tail = pl.multiple_of(to * step + step, LANE)
            for level in range(levels):
                for row in range(rows):
                    low = fields * (rows * level + row)
                    out[low : low + fields, step:] = x_ref[level, row, :, pl.ds(tail, LANE)]

        @pl.when(to == lev_count - 1)
        def _():
            for level in range(levels):
                for row in range(rows):
                    low = fields * (rows * level + row)
                    out[low : low + fields, step : step + last] = x_ref[level, row, :, lev_count * step :]

    copies[-1].wait()
    first = rows * lax.axis_index("lat")
    for row in range(rows):
        whole = lengths_ref[lax.rem(first + row, lengths_ref.shape[0])]
        limit_ref[row : row + 1, :] = jnp.full((1, LANE), whole, jnp.int32)


def turn(multiple, length):
    inverse = 1.0 / length
    rest = multiple - jnp.floor(multiple * inverse) * length
    rest = jnp.where(rest < 0.0, rest + length, rest)
    rest = jnp.where(rest >= length, rest - length, rest)
    quarter = jnp.floor(4.0 * rest * inverse + 0.5)
    angle = (4.0 * rest - quarter * length) * ((TWO_PI / 4.0) * inverse)
    square = angle * angle
    sine = angle + angle * square * (-1.6666654611e-1 + square * (8.3321608736e-3 + square * -1.9515295891e-4))
    cosine = 1.0 - 0.5 * square + square * square * (
        4.166664568298827e-2 + square * (-1.388731625493765e-3 + square * 2.443315711809948e-5)
    )
    odd = (quarter == 1.0) | (quarter == 3.0)
    real = jnp.where(odd, sine, cosine)
    imag = jnp.where(odd, cosine, sine)
    real = jnp.where((quarter == 1.0) | (quarter == 2.0), -real, real)
    imag = jnp.where((quarter == 2.0) | (quarter == 3.0), imag, -imag)
    return real, imag


def table_kernel(limit_ref, wave_ref, after_ref, fine_ref, coarse_ref):
    rows = fine_ref.shape[0]
    waves = wave_ref.shape[1]
    wave = wave_ref[...].astype(jnp.float32)
    coarse_rows = coarse_ref.shape[2]
    small = lax.broadcasted_iota(jnp.int32, (16, 1), 0).astype(jnp.float32)
    blocks = lax.broadcasted_iota(jnp.int32, (coarse_rows, 1), 0).astype(jnp.float32)
    for row in range(rows):
        length = limit_ref[row : row + 1, :1].astype(jnp.float32)
        near_real, near_imag = turn(wave * small, length)
        far_real, far_imag = turn(wave * (16.0 * small), length)
        for part in range(16):
            one_real = far_real[part : part + 1]
            one_imag = far_imag[part : part + 1]
            low = 16 * part
            fine_ref[row, low : low + 16, :waves] = (near_real * one_real - near_imag * one_imag).astype(jnp.bfloat16)
            fine_ref[row, low : low + 16, waves:] = (near_real * one_imag + near_imag * one_real).astype(jnp.bfloat16)
        real, imag = turn(wave * (float(DEEP) * blocks), length)
        scale = jnp.where(2.0 * wave < length, 1.0 / jnp.sqrt(length), 0.0)
        coarse_ref[row, 0] = real * scale
        coarse_ref[row, 1] = imag * scale


def factor_kernel(
    lev_count, points, fields, lower_hbm, upper_hbm, after_ref, first_ref, second_ref, third_ref, lower_ref, upper_ref, sems
):
    block, step, _ = sizes(points, lev_count)
    levels, rows = lower_ref.shape[:2]
    copies = [
        pltpu.make_async_copy(lower_hbm, lower_ref, sems.at[0]),
        pltpu.make_async_copy(upper_hbm, upper_ref, sems.at[1]),
    ]
    for copy in copies:
        copy.start()
    for copy in copies:
        copy.wait()
    me_lev = lax.axis_index("lev")
    own = levels // lev_count
    ratio = None
    for level in range(levels):
        upper = upper_ref[level]
        if level == 0:
            pivot = 1.0 + upper
            above = jnp.zeros_like(upper)
        else:
            diagonal = 1.0 + lower_ref[level]
            if level < levels - 1:
                diagonal = diagonal + upper
            above = upper_ref[level - 1]
            pivot = diagonal + above * ratio
        inverse = 1.0 / pivot
        if level < levels - 1:
            ratio = -lower_ref[level + 1] * inverse
        else:
            ratio = jnp.zeros_like(inverse)
        chunk, inner = divmod(level, own)
        for out, value in ((first_ref, inverse), (second_ref, above * inverse), (third_ref, ratio)):
            for row in range(rows):
                low = fields * (rows * inner + row)
                out[chunk, low : low + fields, :block] = jnp.broadcast_to(value[row : row + 1], (fields, block))
    for out in (first_ref, second_ref, third_ref):
        for chunk in range(out.shape[0]):
            out[chunk] = pltpu.roll(out[chunk], me_lev * (block - step), 1)


def solve_kernel(lev_count, points, fields, limit_ref, first_ref, second_ref, third_ref, *refs):
    block, step, window = sizes(points, lev_count)
    sources, outs, work, done = refs[:lev_count], refs[lev_count : 2 * lev_count], refs[-2], refs[-1]
    rows, members = done.shape[1:3]
    own = members // fields
    levels = lev_count * own
    wide = rows * fields
    me_lev = lax.axis_index("lev")
    for shift, source in enumerate(sources):
        chunk = lax.rem(me_lev + lev_count - shift, lev_count)
        work[chunk] = source[...].astype(jnp.float32)
    lane = lax.broadcasted_iota(jnp.int32, (1, window), 1)
    offset = me_lev * (block - step)
    inside = []
    for row in range(rows):
        whole = limit_ref[row : row + 1, :1]
        inside.append((lane >= offset) & (lane < offset + block) & (lane + me_lev * step < whole))
    part = None
    for level in range(levels):
        chunk, inner = divmod(level, own)
        at = (chunk, slice(wide * inner, wide * (inner + 1)))
        value = work[at] * first_ref[at]
        part = value if part is None else value + second_ref[at] * part
        work[at] = part
    current = None
    for level in range(levels - 1, -1, -1):
        chunk, inner = divmod(level, own)
        at = (chunk, slice(wide * inner, wide * (inner + 1)))
        current = work[at] if current is None else work[at] - third_ref[at] * current
        for row in range(rows):
            done[chunk, row, fields * inner : fields * (inner + 1)] = current[fields * row : fields * (row + 1)]
    for shift, out in enumerate(outs):
        chunk = lax.rem(me_lev + shift, lev_count)
        for row in range(rows):
            out[row] = jnp.where(inside[row], done[chunk, row], 0.0).astype(jnp.bfloat16)


def fourier_kernel(lev_count, points, fine_ref, coarse_ref, *refs):
    _, step, _ = sizes(points, lev_count)
    sources, out_ref, spectra, turned = refs[:lev_count], refs[-3], refs[-2], refs[-1]
    rows = fine_ref.shape[0]
    waves = fine_ref.shape[2] // 2
    per = step // DEEP
    me_lev = lax.axis_index("lev")
    members = sources[0].shape[1]
    final = [lax.rem(me_lev + lev_count - shift, lev_count) == lev_count - 1 for shift in range(lev_count)]
    for row in range(rows):
        tails = [source[row, :, step:] for source in sources]
        none = jnp.zeros_like(tails[0])
        pieces = []
        for shift, source in enumerate(sources):
            before = (shift + 1) % lev_count
            pieces.append(source[row, :, :LANE] + jnp.where(final[before], none, tails[before]))
            pieces[-1] = jnp.concatenate([pieces[-1], source[row, :, LANE:DEEP]], axis=1)
            pieces += [source[row, :, DEEP * a : DEEP * (a + 1)] for a in range(1, per)]
        beyond = none
        for shift in range(lev_count):
            beyond = jnp.where(final[shift], tails[shift], beyond)
        pieces.append(jnp.concatenate([beyond, none], axis=1))
        main = jnp.concatenate(pieces, axis=0)
        for tile in range(waves // DEEP):
            low = DEEP * tile
            main_cos = jnp.dot(main, fine_ref[row, :, low : low + DEEP], preferred_element_type=jnp.float32)
            main_sin = jnp.dot(
                main, fine_ref[row, :, waves + low : waves + low + DEEP], preferred_element_type=jnp.float32
            )
            real = jnp.zeros((members, DEEP), jnp.float32)
            imag = jnp.zeros((members, DEEP), jnp.float32)
            for piece in range(lev_count * per + 1):
                shift, a = divmod(piece, per)
                at = per * lax.rem(me_lev + lev_count - shift, lev_count) + a if shift < lev_count else per * lev_count
                pos = members * piece
                y_cos, y_sin = main_cos[pos : pos + members], main_sin[pos : pos + members]
                c = coarse_ref[row, 0, pl.ds(at, 1), low : low + DEEP]
                s = coarse_ref[row, 1, pl.ds(at, 1), low : low + DEEP]
                real = real + (y_cos * c - y_sin * s)
                imag = imag + (y_sin * c + y_cos * s)
            for half in range(DEEP // LANE):
                at = tile * (DEEP // LANE) + half
                spectra[row, 0, at] = real[:, LANE * half : LANE * (half + 1)]
                spectra[row, 1, at] = imag[:, LANE * half : LANE * (half + 1)]
    for tile in range(waves // LANE):
        low = LANE * tile
        pieces = []
        for row in range(rows):
            one = [
                spectra[row, c, tile, pl.ds(field, members // 2, stride=2), :] for c in range(2) for field in range(2)
            ]
            pieces += one + one
        turned[low : low + LANE, :] = jnp.concatenate(pieces, axis=0).T
    turned[waves:, :] = jnp.zeros((turned.shape[0] - waves, LANE), jnp.float32)
    parts = out_ref.shape[0]
    high = out_ref.shape[1]
    slots = waves // parts
    lane = lax.broadcasted_iota(jnp.int32, (high, LANE), 1)
    left = lax.rem(lane, LANE // 2) < LANE // 4
    for part in range(parts):
        top = turned[slots * part : slots * part + high, :]
        low = turned[slots * part + high : slots * part + 2 * high, :]
        out_ref[part] = jnp.where(left, top, low).astype(jnp.bfloat16)


def pair_kernel(in_ref, out_ref, work, made, sems):
    parts, high = in_ref.shape[:2]
    slots = out_ref.shape[0]
    grid_rows = out_ref.shape[4]
    rows = grid_rows // parts
    for part in range(parts):
        work[high * part : high * (part + 1), :] = in_ref[part].astype(jnp.float32)
    source = lax.broadcasted_iota(jnp.int32, (parts, grid_rows), 0)
    target = lax.broadcasted_iota(jnp.int32, (parts, grid_rows), 1)
    half = grid_rows // 2
    mixes = []
    for row in range(rows):
        place = rows * source + row
        same = lax.rem(place, half) == lax.rem(target, half)
        sign = jnp.where((target >= half) & (place >= half), -1.0, 1.0)
        mixes.append(jnp.where(same, sign, 0.0).astype(jnp.bfloat16))
    half_lanes = LANE // 2
    quarter = half_lanes // 2
    group = 4
    copies = []
    for begin in range(0, high, group):
        turned = [
            work[pl.ds(slot, parts, stride=high), :].T.astype(jnp.bfloat16) for slot in range(begin, begin + group)
        ]
        above = jnp.concatenate([block[:half_lanes] for block in turned], axis=0)
        below = jnp.concatenate([block[half_lanes:] for block in turned], axis=0)
        result = jnp.dot(above, mixes[0], preferred_element_type=jnp.float32)
        result = result + jnp.dot(below, mixes[1], preferred_element_type=jnp.float32)
        for slot in range(group):
            both = result[half_lanes * slot : half_lanes * (slot + 1)]
            made[begin + slot] = both[:quarter].reshape(made.shape[1:])
            if high + begin + slot < slots:
                made[high + begin + slot] = both[quarter:].reshape(made.shape[1:])
        for first in (begin, high + begin):
            if first < slots:
                copy = pltpu.make_async_copy(
                    made.at[first : first + group], out_ref.at[first : first + group], sems.at[len(copies)]
                )
                copy.start()
                copies.append(copy)
    for copy in copies:
        copy.wait()


def near(x):
    return pltpu.with_memory_space_constraint(x, pltpu.VMEM)


def far(x):
    return pltpu.with_memory_space_constraint(x, pltpu.HBM)


def exchange(blocks, order):
    count = lax.axis_size("lev")
    moved = {0: blocks[0]}
    for shift in order:
        moved[shift] = lax.ppermute(blocks[shift], "lev", [(i, (i + shift) % count) for i in range(count)])
    return moved


def body(adjoint_grid, lower_diffusion, upper_diffusion, row_lengths, wave_order):
    lev_count = lax.axis_size("lev")
    lat_count = lax.axis_size("lat")
    levels, rows, fields, points = adjoint_grid.shape
    waves = wave_order.shape[0]
    _, _, window = sizes(points, lev_count)
    f32, bf16 = jnp.float32, jnp.bfloat16
    members = levels * fields
    order = sorted(range(lev_count), key=lambda shift: min(shift, lev_count - shift))
    farthest_first = sorted(order[1:], key=lambda shift: -min(shift, lev_count - shift))
    windows = pltpu.VMEM((rows, members, window), bf16)
    made = pl.pallas_call(
        lambda *refs: pack_kernel(lev_count, order, *refs),
        out_shape=[pltpu.VMEM((rows * members, window), bf16)] * lev_count
        + [pltpu.VMEM((rows, LANE), jnp.int32)],
        in_specs=[ANY] * 2,
        out_specs=[VMEM] * (lev_count + 1),
        scratch_shapes=[
            pltpu.VMEM(adjoint_grid.shape, bf16),
            pltpu.SMEM(row_lengths.shape, jnp.int32),
            pltpu.SemaphoreType.DMA((levels + 1,)),
        ],
        name="pack",
        compiler_params=LIMIT,
    )(far(adjoint_grid), far(row_lengths))
    packed = dict(zip(order, made))
    limit = made[-1]
    arrived = exchange(packed, order[1:])
    factor = pltpu.VMEM((lev_count, rows * members, window), f32)
    factors = pl.pallas_call(
        lambda *refs: factor_kernel(lev_count, points, fields, *refs),
        out_shape=[factor] * 3,
        in_specs=[ANY] * 3,
        out_specs=[VMEM] * 3,
        scratch_shapes=[
            pltpu.VMEM(lower_diffusion.shape, f32),
            pltpu.VMEM(upper_diffusion.shape, f32),
            pltpu.SemaphoreType.DMA((2,)),
        ],
        name="factor",
        compiler_params=LIMIT,
        cost_estimate=pl.CostEstimate(flops=10_000_000, bytes_accessed=4_000_000, transcendentals=0),
    )(far(lower_diffusion), far(upper_diffusion), packed[0])
    solved = pl.pallas_call(
        lambda *refs: solve_kernel(lev_count, points, fields, *refs),
        out_shape=[windows] * lev_count,
        in_specs=[VMEM] * (4 + lev_count),
        out_specs=[VMEM] * lev_count,
        scratch_shapes=[
            pltpu.VMEM((lev_count, rows * members, window), f32),
            pltpu.VMEM((lev_count, rows, members, window), f32),
        ],
        name="solve",
        compiler_params=LIMIT,
    )(near(limit), *[near(x) for x in factors], *[near(arrived[shift]) for shift in range(lev_count)])
    returned = exchange(solved, farthest_first)
    fine, coarse = pl.pallas_call(
        table_kernel,
        out_shape=[pltpu.VMEM((rows, DEEP, 2 * waves), bf16), pltpu.VMEM((rows, 2, 24, waves), f32)],
        in_specs=[VMEM, VMEM, ANY],
        out_specs=[VMEM] * 2,
        name="table",
        compiler_params=LIMIT,
        cost_estimate=pl.CostEstimate(flops=10_000_000, bytes_accessed=4_000_000, transcendentals=0),
    )(near(limit), wave_order[None, :], solved[0])
    slots = waves // lat_count
    high = 24
    sent = pl.pallas_call(
        lambda *refs: fourier_kernel(lev_count, points, *refs),
        out_shape=pltpu.VMEM((lat_count, high, LANE), bf16),
        in_specs=[VMEM] * (2 + lev_count),
        out_specs=VMEM,
        scratch_shapes=[
            pltpu.VMEM((rows, 2, waves // LANE, members, LANE), f32),
            pltpu.VMEM((waves + 16, LANE), f32),
        ],
        name="fourier",
        compiler_params=LIMIT,
    )(near(fine), near(coarse), *[near(returned[shift]) for shift in range(lev_count)])
    received = lax.all_to_all(sent, "lat", split_axis=0, concat_axis=0, tiled=True)
    return pl.pallas_call(
        pair_kernel,
        out_shape=jax.ShapeDtypeStruct((slots, 2, fields, levels, rows * lat_count), f32),
        in_specs=[VMEM],
        out_specs=ANY,
        scratch_shapes=[
            pltpu.VMEM((lat_count * high, LANE), f32),
            pltpu.VMEM((slots, 2, fields, levels, rows * lat_count), f32),
            pltpu.SemaphoreType.DMA((slots // 4,)),
        ],
        name="pair",
        compiler_params=LIMIT,
    )(near(received))


def solution(mesh):
    in_specs = (P("lev", "lat", None, None), P(None, "lat", "lev"), P(None, "lat", "lev"), P(), P())
    out_specs = P("lat", None, None, "lev", None)
    return jax.shard_map(body, mesh=mesh, in_specs=in_specs, out_specs=out_specs, check_vma=False)
```

```python
import jax
import jax.numpy as jnp
from jax import lax
from jax.experimental import pallas as pl
from jax.experimental.pallas import tpu as pltpu
from jax.sharding import PartitionSpec as P

LANE = 128
DEEP = 256
LIMIT = pltpu.CompilerParams(vmem_limit_bytes=24 << 20)
TWO_PI = 6.283185307179586
VMEM = pl.BlockSpec(memory_space=pltpu.VMEM)
ANY = pl.BlockSpec(memory_space=pl.ANY)


def sizes(points, lev_count):
    block = points // lev_count
    step = block // LANE * LANE
    window = step + LANE
    return block, step, window


def pack_kernel(lev_count, shifts, x_hbm, lengths_hbm, *refs):
    outs, (limit_ref, x_ref, lengths_ref, sems) = refs[: len(shifts)], refs[len(shifts) :]
    levels, rows, fields, points = x_ref.shape
    _, step, _ = sizes(points, lev_count)
    last = points - lev_count * step
    me = lax.axis_index("lev")
    pairs = [(x_hbm.at[level], x_ref.at[level]) for level in range(levels)]
    pairs += [(lengths_hbm, lengths_ref)]
    copies = [pltpu.make_async_copy(source, target, sems.at[i]) for i, (source, target) in enumerate(pairs)]
    for copy in copies:
        copy.start()
    pieces = len(copies) - 1
    for piece in range(pieces):
        copies[piece].wait()
        some = range(levels * piece // pieces, levels * (piece + 1) // pieces)
        for shift, out in zip(shifts, outs):
            to = lax.rem(me + shift, lev_count)
            base = pl.multiple_of(to * step, LANE)
            for level in some:
                for row in range(rows):
                    low = fields * (rows * level + row)
                    out[low : low + fields, :step] = x_ref[level, row, :, pl.ds(base, step)]
    for shift, out in zip(shifts, outs):
        to = lax.rem(me + shift, lev_count)

        @pl.when(to < lev_count - 1)
        def _():
            tail = pl.multiple_of(to * step + step, LANE)
            for level in range(levels):
                for row in range(rows):
                    low = fields * (rows * level + row)
                    out[low : low + fields, step:] = x_ref[level, row, :, pl.ds(tail, LANE)]

        @pl.when(to == lev_count - 1)
        def _():
            for level in range(levels):
                for row in range(rows):
                    low = fields * (rows * level + row)
                    out[low : low + fields, step : step + last] = x_ref[level, row, :, lev_count * step :]

    copies[-1].wait()
    first = rows * lax.axis_index("lat")
    for row in range(rows):
        whole = lengths_ref[lax.rem(first + row, lengths_ref.shape[0])]
        limit_ref[row : row + 1, :] = jnp.full((1, LANE), whole, jnp.int32)


def turn(multiple, length):
    inverse = 1.0 / length
    rest = multiple - jnp.floor(multiple * inverse) * length
    rest = jnp.where(rest < 0.0, rest + length, rest)
    rest = jnp.where(rest >= length, rest - length, rest)
    quarter = jnp.floor(4.0 * rest * inverse + 0.5)
    angle = (4.0 * rest - quarter * length) * ((TWO_PI / 4.0) * inverse)
    square = angle * angle
    sine = angle + angle * square * (-1.6666654611e-1 + square * (8.3321608736e-3 + square * -1.9515295891e-4))
    cosine = 1.0 - 0.5 * square + square * square * (
        4.166664568298827e-2 + square * (-1.388731625493765e-3 + square * 2.443315711809948e-5)
    )
    odd = (quarter == 1.0) | (quarter == 3.0)
    real = jnp.where(odd, sine, cosine)
    imag = jnp.where(odd, cosine, sine)
    real = jnp.where((quarter == 1.0) | (quarter == 2.0), -real, real)
    imag = jnp.where((quarter == 2.0) | (quarter == 3.0), imag, -imag)
    return real, imag


def table_kernel(limit_ref, wave_ref, after_ref, fine_ref, coarse_ref):
    rows = fine_ref.shape[0]
    waves = wave_ref.shape[1]
    wave = wave_ref[...].astype(jnp.float32)
    coarse_rows = coarse_ref.shape[2]
    small = lax.broadcasted_iota(jnp.int32, (16, 1), 0).astype(jnp.float32)
    blocks = lax.broadcasted_iota(jnp.int32, (coarse_rows, 1), 0).astype(jnp.float32)
    for row in range(rows):
        length = limit_ref[row : row + 1, :1].astype(jnp.float32)
        near_real, near_imag = turn(wave * small, length)
        far_real, far_imag = turn(wave * (16.0 * small), length)
        for part in range(16):
            one_real = far_real[part : part + 1]
            one_imag = far_imag[part : part + 1]
            low = 16 * part
            fine_ref[row, low : low + 16, :waves] = (near_real * one_real - near_imag * one_imag).astype(jnp.bfloat16)
            fine_ref[row, low : low + 16, waves:] = (near_real * one_imag + near_imag * one_real).astype(jnp.bfloat16)
        real, imag = turn(wave * (float(DEEP) * blocks), length)
        scale = jnp.where(2.0 * wave < length, 1.0 / jnp.sqrt(length), 0.0)
        coarse_ref[row, 0] = real * scale
        coarse_ref[row, 1] = imag * scale


def factor_kernel(
    lev_count, points, fields, lower_hbm, upper_hbm, after_ref, first_ref, second_ref, third_ref, lower_ref, upper_ref, sems
):
    block, step, _ = sizes(points, lev_count)
    levels, rows = lower_ref.shape[:2]
    copies = [
        pltpu.make_async_copy(lower_hbm, lower_ref, sems.at[0]),
        pltpu.make_async_copy(upper_hbm, upper_ref, sems.at[1]),
    ]
    for copy in copies:
        copy.start()
    for copy in copies:
        copy.wait()
    me_lev = lax.axis_index("lev")
    own = levels // lev_count
    ratio = None
    for level in range(levels):
        upper = upper_ref[level]
        if level == 0:
            pivot = 1.0 + upper
            above = jnp.zeros_like(upper)
        else:
            diagonal = 1.0 + lower_ref[level]
            if level < levels - 1:
                diagonal = diagonal + upper
            above = upper_ref[level - 1]
            pivot = diagonal + above * ratio
        inverse = 1.0 / pivot
        if level < levels - 1:
            ratio = -lower_ref[level + 1] * inverse
        else:
            ratio = jnp.zeros_like(inverse)
        chunk, inner = divmod(level, own)
        for out, value in ((first_ref, inverse), (second_ref, above * inverse), (third_ref, ratio)):
            for row in range(rows):
                low = fields * (rows * inner + row)
                out[chunk, low : low + fields, :block] = jnp.broadcast_to(value[row : row + 1], (fields, block))
    for out in (first_ref, second_ref, third_ref):
        for chunk in range(out.shape[0]):
            out[chunk] = pltpu.roll(out[chunk], me_lev * (block - step), 1)


def solve_kernel(lev_count, points, fields, limit_ref, first_ref, second_ref, third_ref, *refs):
    block, step, window = sizes(points, lev_count)
    sources, outs, work, done = refs[:lev_count], refs[lev_count : 2 * lev_count], refs[-2], refs[-1]
    rows, members = done.shape[1:3]
    own = members // fields
    levels = lev_count * own
    wide = rows * fields
    me_lev = lax.axis_index("lev")
    for shift, source in enumerate(sources):
        chunk = lax.rem(me_lev + lev_count - shift, lev_count)
        work[chunk] = source[...].astype(jnp.float32)
    lane = lax.broadcasted_iota(jnp.int32, (1, window), 1)
    offset = me_lev * (block - step)
    inside = []
    for row in range(rows):
        whole = limit_ref[row : row + 1, :1]
        inside.append((lane >= offset) & (lane < offset + block) & (lane + me_lev * step < whole))
    part = None
    for level in range(levels):
        chunk, inner = divmod(level, own)
        at = (chunk, slice(wide * inner, wide * (inner + 1)))
        value = work[at] * first_ref[at]
        part = value if part is None else value + second_ref[at] * part
        work[at] = part
    current = None
    for level in range(levels - 1, -1, -1):
        chunk, inner = divmod(level, own)
        at = (chunk, slice(wide * inner, wide * (inner + 1)))
        current = work[at] if current is None else work[at] - third_ref[at] * current
        for row in range(rows):
            done[chunk, row, fields * inner : fields * (inner + 1)] = current[fields * row : fields * (row + 1)]
    for shift, out in enumerate(outs):
        chunk = lax.rem(me_lev + shift, lev_count)
        for row in range(rows):
            out[row] = jnp.where(inside[row], done[chunk, row], 0.0).astype(jnp.bfloat16)


def blocks_sum(fine_ref, coarse_ref, row, tile, main, places, real, imag):
    waves = fine_ref.shape[2] // 2
    members = main.shape[0] // len(places)
    low = DEEP * tile
    all_cos = jnp.dot(main, fine_ref[row, :, low : low + DEEP], preferred_element_type=jnp.float32)
    all_sin = jnp.dot(main, fine_ref[row, :, waves + low : waves + low + DEEP], preferred_element_type=jnp.float32)
    for piece, place in enumerate(places):
        pos = members * piece
        y_cos, y_sin = all_cos[pos : pos + members], all_sin[pos : pos + members]
        c = coarse_ref[row, 0, pl.ds(place, 1), low : low + DEEP]
        s = coarse_ref[row, 1, pl.ds(place, 1), low : low + DEEP]
        real = real + (y_cos * c - y_sin * s)
        imag = imag + (y_sin * c + y_cos * s)
    return real, imag


def origin_of(shift, count):
    return lax.rem(lax.axis_index("lev") + count - shift, count)


def early_kernel(lev_count, points, shifts, fine_ref, coarse_ref, *refs):
    _, step, _ = sizes(points, lev_count)
    sources, spectra = refs[:-1], refs[-1]
    rows, _, _, members, _ = spectra.shape
    waves = fine_ref.shape[2] // 2
    per = step // DEEP
    places = [per * origin_of(shift, lev_count) + a for shift in shifts for a in range(1, per)]
    for row in range(rows):
        main = jnp.concatenate(
            [source[row, :, DEEP * a : DEEP * (a + 1)] for source in sources for a in range(1, per)], axis=0
        )
        for tile in range(waves // DEEP):
            zero = jnp.zeros((members, DEEP), jnp.float32)
            sums = blocks_sum(fine_ref, coarse_ref, row, tile, main, places, zero, zero)
            for half in range(DEEP // LANE):
                for part, value in enumerate(sums):
                    spectra[row, part, tile * (DEEP // LANE) + half] = value[:, LANE * half : LANE * (half + 1)]


def fourier_kernel(lev_count, points, early, fine_ref, coarse_ref, begun_ref, *refs):
    block, step, _ = sizes(points, lev_count)
    sources, out_ref, spectra, turned = refs[:lev_count], refs[-3], refs[-2], refs[-1]
    rows = fine_ref.shape[0]
    waves = fine_ref.shape[2] // 2
    per = step // DEEP
    final = [origin_of(shift, lev_count) == lev_count - 1 for shift in range(lev_count)]
    places = []
    for shift in range(lev_count):
        places += [per * origin_of(shift, lev_count) + a for a in range(1 if shift in early else per)]
    places.append(per * lev_count)
    for row in range(rows):
        tails = [source[row, :, step:] for source in sources]
        none = jnp.zeros_like(tails[0])
        pieces = []
        for shift, source in enumerate(sources):
            before = (shift + 1) % lev_count
            first = source[row, :, :LANE] + jnp.where(final[before], none, tails[before])
            pieces.append(jnp.concatenate([first, source[row, :, LANE:DEEP]], axis=1))
            if shift not in early:
                pieces += [source[row, :, DEEP * a : DEEP * (a + 1)] for a in range(1, per)]
        beyond = none
        for shift in range(lev_count):
            beyond = jnp.where(final[shift], tails[shift], beyond)
        pieces.append(jnp.concatenate([beyond, none], axis=1))
        main = jnp.concatenate(pieces, axis=0)
        for tile in range(waves // DEEP):
            halves = [tile * (DEEP // LANE) + half for half in range(DEEP // LANE)]
            begun = [jnp.concatenate([begun_ref[row, part, at] for at in halves], axis=1) for part in range(2)]
            sums = blocks_sum(fine_ref, coarse_ref, row, tile, main, places, *begun)
            for half, at in enumerate(halves):
                for part, value in enumerate(sums):
                    spectra[row, part, at] = value[:, LANE * half : LANE * (half + 1)]
    for tile in range(waves // LANE):
        low = LANE * tile
        pieces = []
        for row in range(rows):
            one = [
                spectra[row, c, tile, pl.ds(field, spectra.shape[3] // 2, stride=2), :] for c in range(2) for field in range(2)
            ]
            pieces += one + one
        turned[low : low + LANE, :] = jnp.concatenate(pieces, axis=0).T
    parts, groups, inner = out_ref.shape[:3]
    high = groups * inner
    slots = waves // parts
    lane = lax.broadcasted_iota(jnp.int32, (high, LANE), 1)
    left = lax.rem(lane, LANE // 2) < LANE // 4
    for part in range(parts):
        top = turned[slots * part : slots * part + high, :]
        low = turned[slots * part + high : slots * (part + 1), :]
        block = jnp.where(left, top, low).astype(jnp.bfloat16)
        for group in range(groups):
            out_ref[part, group] = block[inner * group : inner * (group + 1)]


def pair_kernel(in_ref, out_ref, work, made, sems):
    parts, groups, inner = in_ref.shape[:3]
    high = groups * inner
    slots = out_ref.shape[0]
    grid_rows = out_ref.shape[4]
    rows = grid_rows // parts
    for part in range(parts):
        for group in range(groups):
            low = high * part + inner * group
            work[low : low + inner, :] = in_ref[part, group].astype(jnp.float32)
    source = lax.broadcasted_iota(jnp.int32, (parts, grid_rows), 0)
    target = lax.broadcasted_iota(jnp.int32, (parts, grid_rows), 1)
    half = grid_rows // 2
    mixes = []
    for row in range(rows):
        place = rows * source + row
        same = lax.rem(place, half) == lax.rem(target, half)
        sign = jnp.where((target >= half) & (place >= half), -1.0, 1.0)
        mixes.append(jnp.where(same, sign, 0.0).astype(jnp.bfloat16))
    half_lanes = LANE // 2
    quarter = half_lanes // 2
    group = 4
    copies = []
    for begin in range(0, high, group):
        turned = [
            work[pl.ds(slot, parts, stride=high), :].T.astype(jnp.bfloat16) for slot in range(begin, begin + group)
        ]
        above = jnp.concatenate([block[:half_lanes] for block in turned], axis=0)
        below = jnp.concatenate([block[half_lanes:] for block in turned], axis=0)
        result = jnp.dot(above, mixes[0], preferred_element_type=jnp.float32)
        result = result + jnp.dot(below, mixes[1], preferred_element_type=jnp.float32)
        for slot in range(group):
            both = result[half_lanes * slot : half_lanes * (slot + 1)]
            made[begin + slot] = both[:quarter].reshape(made.shape[1:])
            if high + begin + slot < slots:
                made[high + begin + slot] = both[quarter:].reshape(made.shape[1:])
        for first in (begin, high + begin):
            if first < slots:
                copy = pltpu.make_async_copy(
                    made.at[first : first + group], out_ref.at[first : first + group], sems.at[len(copies)]
                )
                copy.start()
                copies.append(copy)
    for copy in copies:
        copy.wait()


def near(x):
    return pltpu.with_memory_space_constraint(x, pltpu.VMEM)


def far(x):
    return pltpu.with_memory_space_constraint(x, pltpu.HBM)


def exchange(blocks, order):
    count = lax.axis_size("lev")
    moved = {0: blocks[0]}
    for shift in order:
        moved[shift] = lax.ppermute(blocks[shift], "lev", [(i, (i + shift) % count) for i in range(count)])
    return moved


def body(adjoint_grid, lower_diffusion, upper_diffusion, row_lengths, wave_order):
    lev_count = lax.axis_size("lev")
    lat_count = lax.axis_size("lat")
    levels, rows, fields, points = adjoint_grid.shape
    waves = wave_order.shape[0]
    _, _, window = sizes(points, lev_count)
    f32, bf16 = jnp.float32, jnp.bfloat16
    members = levels * fields
    order = sorted(range(lev_count), key=lambda shift: min(shift, lev_count - shift))
    farthest_first = sorted(order[1:], key=lambda shift: -min(shift, lev_count - shift))
    windows = pltpu.VMEM((rows, members, window), bf16)
    made = pl.pallas_call(
        lambda *refs: pack_kernel(lev_count, order, *refs),
        out_shape=[pltpu.VMEM((rows * members, window), bf16)] * lev_count
        + [pltpu.VMEM((rows, LANE), jnp.int32)],
        in_specs=[ANY] * 2,
        out_specs=[VMEM] * (lev_count + 1),
        scratch_shapes=[
            pltpu.VMEM(adjoint_grid.shape, bf16),
            pltpu.SMEM(row_lengths.shape, jnp.int32),
            pltpu.SemaphoreType.DMA((levels + 1,)),
        ],
        name="pack",
        compiler_params=LIMIT,
    )(far(adjoint_grid), far(row_lengths))
    packed = dict(zip(order, made))
    limit = made[-1]
    arrived = exchange(packed, order[1:])
    factor = pltpu.VMEM((lev_count, rows * members, window), f32)
    factors = pl.pallas_call(
        lambda *refs: factor_kernel(lev_count, points, fields, *refs),
        out_shape=[factor] * 3,
        in_specs=[ANY] * 3,
        out_specs=[VMEM] * 3,
        scratch_shapes=[
            pltpu.VMEM(lower_diffusion.shape, f32),
            pltpu.VMEM(upper_diffusion.shape, f32),
            pltpu.SemaphoreType.DMA((2,)),
        ],
        name="factor",
        compiler_params=LIMIT,
        cost_estimate=pl.CostEstimate(flops=10_000_000, bytes_accessed=4_000_000, transcendentals=0),
    )(far(lower_diffusion), far(upper_diffusion), packed[0])
    solved = pl.pallas_call(
        lambda *refs: solve_kernel(lev_count, points, fields, *refs),
        out_shape=[windows] * lev_count,
        in_specs=[VMEM] * (4 + lev_count),
        out_specs=[VMEM] * lev_count,
        scratch_shapes=[
            pltpu.VMEM((lev_count, rows * members, window), f32),
            pltpu.VMEM((lev_count, rows, members, window), f32),
        ],
        name="solve",
        compiler_params=LIMIT,
    )(near(limit), *[near(x) for x in factors], *[near(arrived[shift]) for shift in range(lev_count)])
    returned = exchange(solved, farthest_first)
    fine, coarse = pl.pallas_call(
        table_kernel,
        out_shape=[pltpu.VMEM((rows, DEEP, 2 * waves), bf16), pltpu.VMEM((rows, 2, 24, waves), f32)],
        in_specs=[VMEM, VMEM, ANY],
        out_specs=[VMEM] * 2,
        name="table",
        compiler_params=LIMIT,
        cost_estimate=pl.CostEstimate(flops=10_000_000, bytes_accessed=4_000_000, transcendentals=0),
    )(near(limit), wave_order[None, :], solved[0])
    slots = waves // lat_count
    inner = 4
    high = slots // 2
    early = (0, farthest_first[0])
    sums = pltpu.VMEM((rows, 2, waves // LANE, members, LANE), f32)
    begun = pl.pallas_call(
        lambda *refs: early_kernel(lev_count, points, early, *refs),
        out_shape=sums,
        in_specs=[VMEM] * (2 + len(early)),
        out_specs=VMEM,
        name="early",
        cost_estimate=pl.CostEstimate(flops=500_000_000, bytes_accessed=4_000_000, transcendentals=0),
        compiler_params=LIMIT,
    )(near(fine), near(coarse), *[near(returned[shift]) for shift in early])
    sent = pl.pallas_call(
        lambda *refs: fourier_kernel(lev_count, points, early, *refs),
        out_shape=pltpu.VMEM((lat_count, high // inner, inner, LANE), bf16),
        in_specs=[VMEM] * (3 + lev_count),
        out_specs=VMEM,
        scratch_shapes=[sums, pltpu.VMEM((waves, LANE), f32)],
        name="fourier",
        compiler_params=LIMIT,
    )(near(fine), near(coarse), near(begun), *[near(returned[shift]) for shift in range(lev_count)])
    received = lax.all_to_all(sent, "lat", split_axis=0, concat_axis=0, tiled=True)
    return pl.pallas_call(
        pair_kernel,
        out_shape=jax.ShapeDtypeStruct((slots, 2, fields, levels, rows * lat_count), f32),
        in_specs=[VMEM],
        out_specs=ANY,
        scratch_shapes=[
            pltpu.VMEM((lat_count * high, LANE), f32),
            pltpu.VMEM((slots, 2, fields, levels, rows * lat_count), f32),
            pltpu.SemaphoreType.DMA((slots // 4,)),
        ],
        name="pair",
        compiler_params=LIMIT,
    )(near(received))


def solution(mesh):
    in_specs = (P("lev", "lat", None, None), P(None, "lat", "lev"), P(None, "lat", "lev"), P(), P())
    out_specs = P("lat", None, None, "lev", None)
    return jax.shard_map(body, mesh=mesh, in_specs=in_specs, out_specs=out_specs, check_vma=False)
```

```python
import math

import jax
import jax.numpy as jnp
from jax import lax
from jax.experimental import pallas as pl
from jax.experimental.pallas import tpu as pltpu
from jax.sharding import PartitionSpec as P

LANE = 128
DEEP = 256
LIMIT = pltpu.CompilerParams(vmem_limit_bytes=24 << 20)
TWO_PI = 6.283185307179586
VMEM = pl.BlockSpec(memory_space=pltpu.VMEM)
ANY = pl.BlockSpec(memory_space=pl.ANY)


def sizes(points, lev_count):
    block = points // lev_count
    step = block // LANE * LANE
    window = step + LANE
    return block, step, window


def pack_kernel(lev_count, shifts, x_hbm, lengths_hbm, *refs):
    outs, (limit_ref, x_ref, lengths_ref, sems) = refs[: len(shifts)], refs[len(shifts) :]
    levels, rows, fields, points = x_ref.shape
    _, step, _ = sizes(points, lev_count)
    last = points - lev_count * step
    me = lax.axis_index("lev")
    pairs = [(x_hbm.at[level], x_ref.at[level]) for level in range(levels)]
    pairs += [(lengths_hbm, lengths_ref)]
    copies = [pltpu.make_async_copy(source, target, sems.at[i]) for i, (source, target) in enumerate(pairs)]
    for copy in copies:
        copy.start()
    pieces = len(copies) - 1
    for piece in range(pieces):
        copies[piece].wait()
        some = range(levels * piece // pieces, levels * (piece + 1) // pieces)
        for shift, out in zip(shifts, outs):
            to = lax.rem(me + shift, lev_count)
            base = pl.multiple_of(to * step, LANE)
            for level in some:
                for row in range(rows):
                    low = fields * (rows * level + row)
                    out[low : low + fields, :step] = x_ref[level, row, :, pl.ds(base, step)]
    for shift, out in zip(shifts, outs):
        to = lax.rem(me + shift, lev_count)

        @pl.when(to < lev_count - 1)
        def _():
            tail = pl.multiple_of(to * step + step, LANE)
            for level in range(levels):
                for row in range(rows):
                    low = fields * (rows * level + row)
                    out[low : low + fields, step:] = x_ref[level, row, :, pl.ds(tail, LANE)]

        @pl.when(to == lev_count - 1)
        def _():
            for level in range(levels):
                for row in range(rows):
                    low = fields * (rows * level + row)
                    out[low : low + fields, step : step + last] = x_ref[level, row, :, lev_count * step :]

    copies[-1].wait()
    first = rows * lax.axis_index("lat")
    for row in range(rows):
        whole = lengths_ref[lax.rem(first + row, lengths_ref.shape[0])]
        limit_ref[row : row + 1, :] = jnp.full((1, LANE), whole, jnp.int32)


def turn(multiple, length):
    inverse = 1.0 / length
    rest = multiple - jnp.floor(multiple * inverse) * length
    rest = jnp.where(rest < 0.0, rest + length, rest)
    rest = jnp.where(rest >= length, rest - length, rest)
    quarter = jnp.floor(4.0 * rest * inverse + 0.5)
    angle = (4.0 * rest - quarter * length) * ((TWO_PI / 4.0) * inverse)
    square = angle * angle
    sine = angle + angle * square * (-1.6666654611e-1 + square * (8.3321608736e-3 + square * -1.9515295891e-4))
    cosine = 1.0 - 0.5 * square + square * square * (
        4.166664568298827e-2 + square * (-1.388731625493765e-3 + square * 2.443315711809948e-5)
    )
    odd = (quarter == 1.0) | (quarter == 3.0)
    real = jnp.where(odd, sine, cosine)
    imag = jnp.where(odd, cosine, sine)
    real = jnp.where((quarter == 1.0) | (quarter == 2.0), -real, real)
    imag = jnp.where((quarter == 2.0) | (quarter == 3.0), imag, -imag)
    return real, imag


def table_kernel(limit_ref, wave_ref, after_ref, fine_ref, coarse_ref):
    rows = fine_ref.shape[0]
    waves = wave_ref.shape[1]
    wave = wave_ref[...].astype(jnp.float32)
    coarse_rows = coarse_ref.shape[2]
    small = lax.broadcasted_iota(jnp.int32, (16, 1), 0).astype(jnp.float32)
    blocks = lax.broadcasted_iota(jnp.int32, (coarse_rows, 1), 0).astype(jnp.float32)
    for row in range(rows):
        length = limit_ref[row : row + 1, :1].astype(jnp.float32)
        near_real, near_imag = turn(wave * small, length)
        far_real, far_imag = turn(wave * (16.0 * small), length)
        for part in range(16):
            one_real = far_real[part : part + 1]
            one_imag = far_imag[part : part + 1]
            low = 16 * part
            fine_ref[row, low : low + 16, :waves] = (near_real * one_real - near_imag * one_imag).astype(jnp.bfloat16)
            fine_ref[row, low : low + 16, waves:] = (near_real * one_imag + near_imag * one_real).astype(jnp.bfloat16)
        real, imag = turn(wave * (float(DEEP) * blocks), length)
        scale = jnp.where(2.0 * wave < length, 1.0 / jnp.sqrt(length), 0.0)
        coarse_ref[row, 0] = real * scale
        coarse_ref[row, 1] = imag * scale


def factor_kernel(
    lev_count, points, fields, lower_hbm, upper_hbm, after_ref, first_ref, second_ref, third_ref, lower_ref, upper_ref, sems
):
    block, step, _ = sizes(points, lev_count)
    levels, rows = lower_ref.shape[:2]
    copies = [
        pltpu.make_async_copy(lower_hbm, lower_ref, sems.at[0]),
        pltpu.make_async_copy(upper_hbm, upper_ref, sems.at[1]),
    ]
    for copy in copies:
        copy.start()
    for copy in copies:
        copy.wait()
    me_lev = lax.axis_index("lev")
    own = levels // lev_count
    ratio = None
    for level in range(levels):
        upper = upper_ref[level]
        if level == 0:
            pivot = 1.0 + upper
            above = jnp.zeros_like(upper)
        else:
            diagonal = 1.0 + lower_ref[level]
            if level < levels - 1:
                diagonal = diagonal + upper
            above = upper_ref[level - 1]
            pivot = diagonal + above * ratio
        inverse = 1.0 / pivot
        if level < levels - 1:
            ratio = -lower_ref[level + 1] * inverse
        else:
            ratio = jnp.zeros_like(inverse)
        chunk, inner = divmod(level, own)
        for out, value in ((first_ref, inverse), (second_ref, above * inverse), (third_ref, ratio)):
            for row in range(rows):
                low = fields * (rows * inner + row)
                out[chunk, low : low + fields, :block] = jnp.broadcast_to(value[row : row + 1], (fields, block))
    for out in (first_ref, second_ref, third_ref):
        for chunk in range(out.shape[0]):
            out[chunk] = pltpu.roll(out[chunk], me_lev * (block - step), 1)


def solve_kernel(lev_count, points, fields, limit_ref, first_ref, second_ref, third_ref, *refs):
    block, step, window = sizes(points, lev_count)
    sources, outs, work, done = refs[:lev_count], refs[lev_count : 2 * lev_count], refs[-2], refs[-1]
    rows, members = done.shape[1:3]
    own = members // fields
    levels = lev_count * own
    wide = rows * fields
    me_lev = lax.axis_index("lev")
    for shift, source in enumerate(sources):
        chunk = lax.rem(me_lev + lev_count - shift, lev_count)
        work[chunk] = source[...].astype(jnp.float32)
    lane = lax.broadcasted_iota(jnp.int32, (1, window), 1)
    offset = me_lev * (block - step)
    inside = []
    for row in range(rows):
        whole = limit_ref[row : row + 1, :1]
        inside.append((lane >= offset) & (lane < offset + block) & (lane + me_lev * step < whole))
    part = None
    for level in range(levels):
        chunk, inner = divmod(level, own)
        at = (chunk, slice(wide * inner, wide * (inner + 1)))
        value = work[at] * first_ref[at]
        part = value if part is None else value + second_ref[at] * part
        work[at] = part
    current = None
    for level in range(levels - 1, -1, -1):
        chunk, inner = divmod(level, own)
        at = (chunk, slice(wide * inner, wide * (inner + 1)))
        current = work[at] if current is None else work[at] - third_ref[at] * current
        for row in range(rows):
            done[chunk, row, fields * inner : fields * (inner + 1)] = current[fields * row : fields * (row + 1)]
    for shift, out in enumerate(outs):
        chunk = lax.rem(me_lev + shift, lev_count)
        for row in range(rows):
            out[row] = jnp.where(inside[row], done[chunk, row], 0.0).astype(jnp.bfloat16)


def blocks_sum(fine_ref, coarse_ref, row, tile, main, places, real, imag):
    waves = fine_ref.shape[2] // 2
    members = main.shape[0] // len(places)
    low = DEEP * tile
    all_cos = jnp.dot(main, fine_ref[row, :, low : low + DEEP], preferred_element_type=jnp.float32)
    all_sin = jnp.dot(main, fine_ref[row, :, waves + low : waves + low + DEEP], preferred_element_type=jnp.float32)
    for piece, place in enumerate(places):
        pos = members * piece
        y_cos, y_sin = all_cos[pos : pos + members], all_sin[pos : pos + members]
        c = coarse_ref[row, 0, pl.ds(place, 1), low : low + DEEP]
        s = coarse_ref[row, 1, pl.ds(place, 1), low : low + DEEP]
        real = real + (y_cos * c - y_sin * s)
        imag = imag + (y_sin * c + y_cos * s)
    return real, imag


def origin_of(shift, count):
    return lax.rem(lax.axis_index("lev") + count - shift, count)


def early_kernel(lev_count, points, shifts, fine_ref, coarse_ref, *refs):
    _, step, _ = sizes(points, lev_count)
    sources, spectra = refs[:-1], refs[-1]
    rows, _, _, members, _ = spectra.shape
    waves = fine_ref.shape[2] // 2
    per = step // DEEP
    places = [per * origin_of(shift, lev_count) + a for shift in shifts for a in range(1, per)]
    for row in range(rows):
        main = jnp.concatenate(
            [source[row, :, DEEP * a : DEEP * (a + 1)] for source in sources for a in range(1, per)], axis=0
        )
        for tile in range(waves // DEEP):
            zero = jnp.zeros((members, DEEP), jnp.float32)
            sums = blocks_sum(fine_ref, coarse_ref, row, tile, main, places, zero, zero)
            for half in range(DEEP // LANE):
                for part, value in enumerate(sums):
                    spectra[row, part, tile * (DEEP // LANE) + half] = value[:, LANE * half : LANE * (half + 1)]


def fourier_kernel(lev_count, points, early, order, fine_ref, coarse_ref, begun_ref, *refs):
    block, step, _ = sizes(points, lev_count)
    sources, out_ref, spectra, turned = refs[:lev_count], refs[-3], refs[-2], refs[-1]
    rows = fine_ref.shape[0]
    waves = fine_ref.shape[2] // 2
    per = step // DEEP
    final = [origin_of(shift, lev_count) == lev_count - 1 for shift in range(lev_count)]
    places = []
    for shift in range(lev_count):
        places += [per * origin_of(shift, lev_count) + a for a in range(1 if shift in early else per)]
    places.append(per * lev_count)
    for row in range(rows):
        tails = [source[row, :, step:] for source in sources]
        none = jnp.zeros_like(tails[0])
        pieces = []
        for shift, source in enumerate(sources):
            before = (shift + 1) % lev_count
            first = source[row, :, :LANE] + jnp.where(final[before], none, tails[before])
            pieces.append(jnp.concatenate([first, source[row, :, LANE:DEEP]], axis=1))
            if shift not in early:
                pieces += [source[row, :, DEEP * a : DEEP * (a + 1)] for a in range(1, per)]
        beyond = none
        for shift in range(lev_count):
            beyond = jnp.where(final[shift], tails[shift], beyond)
        pieces.append(jnp.concatenate([beyond, none], axis=1))
        main = jnp.concatenate(pieces, axis=0)
        for tile in range(waves // DEEP):
            halves = [tile * (DEEP // LANE) + half for half in range(DEEP // LANE)]
            begun = [jnp.concatenate([begun_ref[row, part, at] for at in halves], axis=1) for part in range(2)]
            sums = blocks_sum(fine_ref, coarse_ref, row, tile, main, places, *begun)
            for half, at in enumerate(halves):
                for part, value in enumerate(sums):
                    spectra[row, part, at] = value[:, LANE * half : LANE * (half + 1)]
    for tile in range(waves // LANE):
        low = LANE * tile
        pieces = []
        for row in range(rows):
            one = [
                spectra[row, c, tile, pl.ds(field, spectra.shape[3] // 2, stride=2), :] for c in range(2) for field in range(2)
            ]
            pieces += one + one
        turned[low : low + LANE, :] = jnp.concatenate(pieces, axis=0).T
    parts, groups, inner = out_ref.shape[:3]
    high = groups * inner
    slots = waves // parts
    lane = lax.broadcasted_iota(jnp.int32, (high, LANE), 1)
    left = lax.rem(lane, LANE // 2) < LANE // 4
    for place, part in enumerate(order):
        top = turned[slots * part : slots * part + high, :]
        low = turned[slots * part + high : slots * (part + 1), :]
        block = jnp.where(left, top, low).astype(jnp.bfloat16)
        for group in range(groups):
            out_ref[place, group] = block[inner * group : inner * (group + 1)]


def pair_kernel(order, in_ref, out_ref, work, made, sems):
    parts, groups, inner = in_ref.shape[:3]
    high = groups * inner
    slots = out_ref.shape[0]
    grid_rows = out_ref.shape[4]
    rows = grid_rows // parts
    for place, part in enumerate(order):
        for group in range(groups):
            low = high * part + inner * group
            work[low : low + inner, :] = in_ref[place, group].astype(jnp.float32)
    source = lax.broadcasted_iota(jnp.int32, (parts, grid_rows), 0)
    target = lax.broadcasted_iota(jnp.int32, (parts, grid_rows), 1)
    half = grid_rows // 2
    mixes = []
    for row in range(rows):
        place = rows * source + row
        same = lax.rem(place, half) == lax.rem(target, half)
        sign = jnp.where((target >= half) & (place >= half), -1.0, 1.0)
        mixes.append(jnp.where(same, sign, 0.0).astype(jnp.bfloat16))
    half_lanes = LANE // 2
    quarter = half_lanes // 2
    group = 4
    copies = []
    for begin in range(0, high, group):
        turned = [
            work[pl.ds(slot, parts, stride=high), :].T.astype(jnp.bfloat16) for slot in range(begin, begin + group)
        ]
        above = jnp.concatenate([block[:half_lanes] for block in turned], axis=0)
        below = jnp.concatenate([block[half_lanes:] for block in turned], axis=0)
        result = jnp.dot(above, mixes[0], preferred_element_type=jnp.float32)
        result = result + jnp.dot(below, mixes[1], preferred_element_type=jnp.float32)
        for slot in range(group):
            both = result[half_lanes * slot : half_lanes * (slot + 1)]
            made[begin + slot] = both[:quarter].reshape(made.shape[1:])
            if high + begin + slot < slots:
                made[high + begin + slot] = both[quarter:].reshape(made.shape[1:])
        for first in (begin, high + begin):
            if first < slots:
                copy = pltpu.make_async_copy(
                    made.at[first : first + group], out_ref.at[first : first + group], sems.at[len(copies)]
                )
                copy.start()
                copies.append(copy)
    for copy in copies:
        copy.wait()


def middle_first(count):
    cores = 2
    side = math.isqrt(count // cores)
    half = side // 2
    return [
        ((i // (side * cores) + half) % side * side + (i // cores + half) % side) * cores + cores - 1 - i % cores
        for i in range(count)
    ]


def near(x):
    return pltpu.with_memory_space_constraint(x, pltpu.VMEM)


def far(x):
    return pltpu.with_memory_space_constraint(x, pltpu.HBM)


def exchange(blocks, order):
    count = lax.axis_size("lev")
    moved = {0: blocks[0]}
    for shift in order:
        moved[shift] = lax.ppermute(blocks[shift], "lev", [(i, (i + shift) % count) for i in range(count)])
    return moved


def body(adjoint_grid, lower_diffusion, upper_diffusion, row_lengths, wave_order):
    lev_count = lax.axis_size("lev")
    lat_count = lax.axis_size("lat")
    levels, rows, fields, points = adjoint_grid.shape
    waves = wave_order.shape[0]
    _, _, window = sizes(points, lev_count)
    f32, bf16 = jnp.float32, jnp.bfloat16
    members = levels * fields
    order = sorted(range(lev_count), key=lambda shift: min(shift, lev_count - shift))
    farthest_first = sorted(order[1:], key=lambda shift: -min(shift, lev_count - shift))
    windows = pltpu.VMEM((rows, members, window), bf16)
    made = pl.pallas_call(
        lambda *refs: pack_kernel(lev_count, order, *refs),
        out_shape=[pltpu.VMEM((rows * members, window), bf16)] * lev_count
        + [pltpu.VMEM((rows, LANE), jnp.int32)],
        in_specs=[ANY] * 2,
        out_specs=[VMEM] * (lev_count + 1),
        scratch_shapes=[
            pltpu.VMEM(adjoint_grid.shape, bf16),
            pltpu.SMEM(row_lengths.shape, jnp.int32),
            pltpu.SemaphoreType.DMA((levels + 1,)),
        ],
        name="pack",
        compiler_params=LIMIT,
    )(far(adjoint_grid), far(row_lengths))
    packed = dict(zip(order, made))
    limit = made[-1]
    arrived = exchange(packed, order[1:])
    factor = pltpu.VMEM((lev_count, rows * members, window), f32)
    factors = pl.pallas_call(
        lambda *refs: factor_kernel(lev_count, points, fields, *refs),
        out_shape=[factor] * 3,
        in_specs=[ANY] * 3,
        out_specs=[VMEM] * 3,
        scratch_shapes=[
            pltpu.VMEM(lower_diffusion.shape, f32),
            pltpu.VMEM(upper_diffusion.shape, f32),
            pltpu.SemaphoreType.DMA((2,)),
        ],
        name="factor",
        compiler_params=LIMIT,
        cost_estimate=pl.CostEstimate(flops=10_000_000, bytes_accessed=4_000_000, transcendentals=0),
    )(far(lower_diffusion), far(upper_diffusion), packed[0])
    solved = pl.pallas_call(
        lambda *refs: solve_kernel(lev_count, points, fields, *refs),
        out_shape=[windows] * lev_count,
        in_specs=[VMEM] * (4 + lev_count),
        out_specs=[VMEM] * lev_count,
        scratch_shapes=[
            pltpu.VMEM((lev_count, rows * members, window), f32),
            pltpu.VMEM((lev_count, rows, members, window), f32),
        ],
        name="solve",
        compiler_params=LIMIT,
    )(near(limit), *[near(x) for x in factors], *[near(arrived[shift]) for shift in range(lev_count)])
    returned = exchange(solved, farthest_first)
    fine, coarse = pl.pallas_call(
        table_kernel,
        out_shape=[pltpu.VMEM((rows, DEEP, 2 * waves), bf16), pltpu.VMEM((rows, 2, 24, waves), f32)],
        in_specs=[VMEM, VMEM, ANY],
        out_specs=[VMEM] * 2,
        name="table",
        compiler_params=LIMIT,
        cost_estimate=pl.CostEstimate(flops=10_000_000, bytes_accessed=4_000_000, transcendentals=0),
    )(near(limit), wave_order[None, :], solved[0])
    slots = waves // lat_count
    inner = 4
    high = slots // 2
    early = (0, farthest_first[0])
    members_order = middle_first(lat_count)
    sums = pltpu.VMEM((rows, 2, waves // LANE, members, LANE), f32)
    begun = pl.pallas_call(
        lambda *refs: early_kernel(lev_count, points, early, *refs),
        out_shape=sums,
        in_specs=[VMEM] * (2 + len(early)),
        out_specs=VMEM,
        name="early",
        cost_estimate=pl.CostEstimate(flops=500_000_000, bytes_accessed=4_000_000, transcendentals=0),
        compiler_params=LIMIT,
    )(near(fine), near(coarse), *[near(returned[shift]) for shift in early])
    sent = pl.pallas_call(
        lambda *refs: fourier_kernel(lev_count, points, early, members_order, *refs),
        out_shape=pltpu.VMEM((lat_count, high // inner, inner, LANE), bf16),
        in_specs=[VMEM] * (3 + lev_count),
        out_specs=VMEM,
        scratch_shapes=[sums, pltpu.VMEM((waves, LANE), f32)],
        name="fourier",
        compiler_params=LIMIT,
    )(near(fine), near(coarse), near(begun), *[near(returned[shift]) for shift in range(lev_count)])
    received = lax.all_to_all(
        sent, "lat", split_axis=0, concat_axis=0, tiled=True, axis_index_groups=[members_order]
    )
    return pl.pallas_call(
        lambda *refs: pair_kernel(members_order, *refs),
        out_shape=jax.ShapeDtypeStruct((slots, 2, fields, levels, rows * lat_count), f32),
        in_specs=[VMEM],
        out_specs=ANY,
        scratch_shapes=[
            pltpu.VMEM((lat_count * high, LANE), f32),
            pltpu.VMEM((slots, 2, fields, levels, rows * lat_count), f32),
            pltpu.SemaphoreType.DMA((slots // 4,)),
        ],
        name="pair",
        compiler_params=LIMIT,
    )(near(received))


def solution(mesh):
    in_specs = (P("lev", "lat", None, None), P(None, "lat", "lev"), P(None, "lat", "lev"), P(), P())
    out_specs = P("lat", None, None, "lev", None)
    return jax.shard_map(body, mesh=mesh, in_specs=in_specs, out_specs=out_specs, check_vma=False)
```

```python
import math

import jax
import jax.numpy as jnp
from jax import lax
from jax.experimental import pallas as pl
from jax.experimental.pallas import tpu as pltpu
from jax.sharding import PartitionSpec as P

LANE = 128
DEEP = 256
LIMIT = pltpu.CompilerParams(vmem_limit_bytes=24 << 20)
TWO_PI = 6.283185307179586
VMEM = pl.BlockSpec(memory_space=pltpu.VMEM)
ANY = pl.BlockSpec(memory_space=pl.ANY)


def sizes(points, lev_count):
    block = points // lev_count
    step = block // LANE * LANE
    window = step + LANE
    return block, step, window


def pack_kernel(lev_count, shifts, x_hbm, lengths_hbm, *refs):
    outs, (limit_ref, x_ref, lengths_ref, sems) = refs[: len(shifts)], refs[len(shifts) :]
    levels, rows, fields, points = x_ref.shape
    _, step, _ = sizes(points, lev_count)
    last = points - lev_count * step
    me = lax.axis_index("lev")
    pairs = [(x_hbm.at[level], x_ref.at[level]) for level in range(levels)]
    pairs += [(lengths_hbm, lengths_ref)]
    copies = [pltpu.make_async_copy(source, target, sems.at[i]) for i, (source, target) in enumerate(pairs)]
    for copy in copies:
        copy.start()
    pieces = len(copies) - 1
    for piece in range(pieces):
        copies[piece].wait()
        some = range(levels * piece // pieces, levels * (piece + 1) // pieces)
        for shift, out in zip(shifts, outs):
            to = lax.rem(me + shift, lev_count)
            base = pl.multiple_of(to * step, LANE)
            for level in some:
                for row in range(rows):
                    low = fields * (rows * level + row)
                    out[low : low + fields, :step] = x_ref[level, row, :, pl.ds(base, step)]
    for shift, out in zip(shifts, outs):
        to = lax.rem(me + shift, lev_count)

        @pl.when(to < lev_count - 1)
        def _():
            tail = pl.multiple_of(to * step + step, LANE)
            for level in range(levels):
                for row in range(rows):
                    low = fields * (rows * level + row)
                    out[low : low + fields, step:] = x_ref[level, row, :, pl.ds(tail, LANE)]

        @pl.when(to == lev_count - 1)
        def _():
            for level in range(levels):
                for row in range(rows):
                    low = fields * (rows * level + row)
                    out[low : low + fields, step : step + last] = x_ref[level, row, :, lev_count * step :]

    copies[-1].wait()
    first = rows * lax.axis_index("lat")
    for row in range(rows):
        whole = lengths_ref[lax.rem(first + row, lengths_ref.shape[0])]
        limit_ref[row : row + 1, :] = jnp.full((1, LANE), whole, jnp.int32)


def turn(multiple, length):
    inverse = 1.0 / length
    rest = multiple - jnp.floor(multiple * inverse) * length
    rest = jnp.where(rest < 0.0, rest + length, rest)
    rest = jnp.where(rest >= length, rest - length, rest)
    quarter = jnp.floor(4.0 * rest * inverse + 0.5)
    angle = (4.0 * rest - quarter * length) * ((TWO_PI / 4.0) * inverse)
    square = angle * angle
    sine = angle + angle * square * (-1.6666654611e-1 + square * (8.3321608736e-3 + square * -1.9515295891e-4))
    cosine = 1.0 - 0.5 * square + square * square * (
        4.166664568298827e-2 + square * (-1.388731625493765e-3 + square * 2.443315711809948e-5)
    )
    odd = (quarter == 1.0) | (quarter == 3.0)
    real = jnp.where(odd, sine, cosine)
    imag = jnp.where(odd, cosine, sine)
    real = jnp.where((quarter == 1.0) | (quarter == 2.0), -real, real)
    imag = jnp.where((quarter == 2.0) | (quarter == 3.0), imag, -imag)
    return real, imag


def table_kernel(limit_ref, wave_ref, after_ref, fine_ref, coarse_ref):
    rows = fine_ref.shape[0]
    waves = wave_ref.shape[1]
    wave = wave_ref[...].astype(jnp.float32)
    coarse_rows = coarse_ref.shape[2]
    small = lax.broadcasted_iota(jnp.int32, (16, 1), 0).astype(jnp.float32)
    blocks = lax.broadcasted_iota(jnp.int32, (coarse_rows, 1), 0).astype(jnp.float32)
    for row in range(rows):
        length = limit_ref[row : row + 1, :1].astype(jnp.float32)
        near_real, near_imag = turn(wave * small, length)
        far_real, far_imag = turn(wave * (16.0 * small), length)
        for part in range(16):
            one_real = far_real[part : part + 1]
            one_imag = far_imag[part : part + 1]
            low = 16 * part
            fine_ref[row, low : low + 16, :waves] = (near_real * one_real - near_imag * one_imag).astype(jnp.bfloat16)
            fine_ref[row, low : low + 16, waves:] = (near_real * one_imag + near_imag * one_real).astype(jnp.bfloat16)
        real, imag = turn(wave * (float(DEEP) * blocks), length)
        scale = jnp.where(2.0 * wave < length, 1.0 / jnp.sqrt(length), 0.0)
        coarse_ref[row, 0] = real * scale
        coarse_ref[row, 1] = imag * scale


def factor_kernel(
    lev_count, points, fields, lower_hbm, upper_hbm, after_ref, first_ref, second_ref, third_ref, lower_ref, upper_ref, sems
):
    block, step, _ = sizes(points, lev_count)
    levels, rows = lower_ref.shape[:2]
    copies = [
        pltpu.make_async_copy(lower_hbm, lower_ref, sems.at[0]),
        pltpu.make_async_copy(upper_hbm, upper_ref, sems.at[1]),
    ]
    for copy in copies:
        copy.start()
    for copy in copies:
        copy.wait()
    me_lev = lax.axis_index("lev")
    own = levels // lev_count
    ratio = None
    for level in range(levels):
        upper = upper_ref[level]
        if level == 0:
            pivot = 1.0 + upper
            above = jnp.zeros_like(upper)
        else:
            diagonal = 1.0 + lower_ref[level]
            if level < levels - 1:
                diagonal = diagonal + upper
            above = upper_ref[level - 1]
            pivot = diagonal + above * ratio
        inverse = 1.0 / pivot
        if level < levels - 1:
            ratio = -lower_ref[level + 1] * inverse
        else:
            ratio = jnp.zeros_like(inverse)
        chunk, inner = divmod(level, own)
        for out, value in ((first_ref, inverse), (second_ref, above * inverse), (third_ref, ratio)):
            for row in range(rows):
                low = fields * (rows * inner + row)
                out[chunk, low : low + fields, :block] = jnp.broadcast_to(value[row : row + 1], (fields, block))
    for out in (first_ref, second_ref, third_ref):
        for chunk in range(out.shape[0]):
            out[chunk] = pltpu.roll(out[chunk], me_lev * (block - step), 1)


def solve_kernel(lev_count, points, fields, limit_ref, first_ref, second_ref, third_ref, *refs):
    block, step, window = sizes(points, lev_count)
    sources, outs, work, done = refs[:lev_count], refs[lev_count : 2 * lev_count], refs[-2], refs[-1]
    rows, members = done.shape[1:3]
    own = members // fields
    levels = lev_count * own
    wide = rows * fields
    me_lev = lax.axis_index("lev")
    for shift, source in enumerate(sources):
        chunk = lax.rem(me_lev + lev_count - shift, lev_count)
        work[chunk] = source[...].astype(jnp.float32)
    lane = lax.broadcasted_iota(jnp.int32, (1, window), 1)
    offset = me_lev * (block - step)
    inside = []
    for row in range(rows):
        whole = limit_ref[row : row + 1, :1]
        inside.append((lane >= offset) & (lane < offset + block) & (lane + me_lev * step < whole))
    part = None
    for level in range(levels):
        chunk, inner = divmod(level, own)
        at = (chunk, slice(wide * inner, wide * (inner + 1)))
        value = work[at] * first_ref[at]
        part = value if part is None else value + second_ref[at] * part
        work[at] = part
    current = None
    for level in range(levels - 1, -1, -1):
        chunk, inner = divmod(level, own)
        at = (chunk, slice(wide * inner, wide * (inner + 1)))
        current = work[at] if current is None else work[at] - third_ref[at] * current
        for row in range(rows):
            done[chunk, row, fields * inner : fields * (inner + 1)] = current[fields * row : fields * (row + 1)]
    for shift, out in enumerate(outs):
        chunk = lax.rem(me_lev + shift, lev_count)
        for row in range(rows):
            out[row] = jnp.where(inside[row], done[chunk, row], 0.0).astype(jnp.bfloat16)


def blocks_sum(fine_ref, coarse_ref, row, tile, main, places, real, imag):
    waves = fine_ref.shape[2] // 2
    members = main.shape[0] // len(places)
    low = DEEP * tile
    all_cos = jnp.dot(main, fine_ref[row, :, low : low + DEEP], preferred_element_type=jnp.float32)
    all_sin = jnp.dot(main, fine_ref[row, :, waves + low : waves + low + DEEP], preferred_element_type=jnp.float32)
    for piece, place in enumerate(places):
        pos = members * piece
        y_cos, y_sin = all_cos[pos : pos + members], all_sin[pos : pos + members]
        c = coarse_ref[row, 0, pl.ds(place, 1), low : low + DEEP]
        s = coarse_ref[row, 1, pl.ds(place, 1), low : low + DEEP]
        real = real + (y_cos * c - y_sin * s)
        imag = imag + (y_sin * c + y_cos * s)
    return real, imag


def origin_of(shift, count):
    return lax.rem(lax.axis_index("lev") + count - shift, count)


def early_kernel(lev_count, points, shifts, fine_ref, coarse_ref, *refs):
    _, step, _ = sizes(points, lev_count)
    sources, begun, spectra = refs[: len(shifts)], refs[len(shifts) : -1], refs[-1]
    rows, _, _, members, _ = spectra.shape
    waves = fine_ref.shape[2] // 2
    per = step // DEEP
    places = [per * origin_of(shift, lev_count) + a for shift in shifts for a in range(1, per)]
    for row in range(rows):
        main = jnp.concatenate(
            [source[row, :, DEEP * a : DEEP * (a + 1)] for source in sources for a in range(1, per)], axis=0
        )
        for tile in range(waves // DEEP):
            halves = [tile * (DEEP // LANE) + half for half in range(DEEP // LANE)]
            before = [jnp.zeros((members, DEEP), jnp.float32)] * 2
            for ref in begun:
                before = [jnp.concatenate([ref[row, part, at] for at in halves], axis=1) for part in range(2)]
            sums = blocks_sum(fine_ref, coarse_ref, row, tile, main, places, *before)
            for half in range(DEEP // LANE):
                for part, value in enumerate(sums):
                    spectra[row, part, tile * (DEEP // LANE) + half] = value[:, LANE * half : LANE * (half + 1)]


def fourier_kernel(lev_count, points, early, order, fine_ref, coarse_ref, begun_ref, *refs):
    block, step, _ = sizes(points, lev_count)
    sources, out_ref, spectra, turned = refs[:lev_count], refs[-3], refs[-2], refs[-1]
    rows = fine_ref.shape[0]
    waves = fine_ref.shape[2] // 2
    per = step // DEEP
    final = [origin_of(shift, lev_count) == lev_count - 1 for shift in range(lev_count)]
    places = []
    for shift in range(lev_count):
        places += [per * origin_of(shift, lev_count) + a for a in range(1 if shift in early else per)]
    places.append(per * lev_count)
    for row in range(rows):
        tails = [source[row, :, step:] for source in sources]
        none = jnp.zeros_like(tails[0])
        pieces = []
        for shift, source in enumerate(sources):
            before = (shift + 1) % lev_count
            first = source[row, :, :LANE] + jnp.where(final[before], none, tails[before])
            pieces.append(jnp.concatenate([first, source[row, :, LANE:DEEP]], axis=1))
            if shift not in early:
                pieces += [source[row, :, DEEP * a : DEEP * (a + 1)] for a in range(1, per)]
        beyond = none
        for shift in range(lev_count):
            beyond = jnp.where(final[shift], tails[shift], beyond)
        pieces.append(jnp.concatenate([beyond, none], axis=1))
        main = jnp.concatenate(pieces, axis=0)
        for tile in range(waves // DEEP):
            halves = [tile * (DEEP // LANE) + half for half in range(DEEP // LANE)]
            begun = [jnp.concatenate([begun_ref[row, part, at] for at in halves], axis=1) for part in range(2)]
            sums = blocks_sum(fine_ref, coarse_ref, row, tile, main, places, *begun)
            for half, at in enumerate(halves):
                for part, value in enumerate(sums):
                    spectra[row, part, at] = value[:, LANE * half : LANE * (half + 1)]
    for tile in range(waves // LANE):
        low = LANE * tile
        pieces = []
        for row in range(rows):
            one = [
                spectra[row, c, tile, pl.ds(field, spectra.shape[3] // 2, stride=2), :] for c in range(2) for field in range(2)
            ]
            pieces += one + one
        turned[low : low + LANE, :] = jnp.concatenate(pieces, axis=0).T
    parts, groups, inner = out_ref.shape[:3]
    high = groups * inner
    slots = waves // parts
    lane = lax.broadcasted_iota(jnp.int32, (high, LANE), 1)
    left = lax.rem(lane, LANE // 2) < LANE // 4
    for place, part in enumerate(order):
        top = turned[slots * part : slots * part + high, :]
        low = turned[slots * part + high : slots * (part + 1), :]
        block = jnp.where(left, top, low).astype(jnp.bfloat16)
        for group in range(groups):
            out_ref[place, group] = block[inner * group : inner * (group + 1)]


def pair_kernel(order, in_ref, out_ref, work, made, sems):
    parts, groups, inner = in_ref.shape[:3]
    high = groups * inner
    slots = out_ref.shape[0]
    grid_rows = out_ref.shape[4]
    rows = grid_rows // parts
    for place, part in enumerate(order):
        for group in range(groups):
            low = high * part + inner * group
            work[low : low + inner, :] = in_ref[place, group].astype(jnp.float32)
    source = lax.broadcasted_iota(jnp.int32, (parts, grid_rows), 0)
    target = lax.broadcasted_iota(jnp.int32, (parts, grid_rows), 1)
    half = grid_rows // 2
    mixes = []
    for row in range(rows):
        place = rows * source + row
        same = lax.rem(place, half) == lax.rem(target, half)
        sign = jnp.where((target >= half) & (place >= half), -1.0, 1.0)
        mixes.append(jnp.where(same, sign, 0.0).astype(jnp.bfloat16))
    half_lanes = LANE // 2
    quarter = half_lanes // 2
    group = 4
    copies = []
    for begin in range(0, high, group):
        turned = [
            work[pl.ds(slot, parts, stride=high), :].T.astype(jnp.bfloat16) for slot in range(begin, begin + group)
        ]
        above = jnp.concatenate([block[:half_lanes] for block in turned], axis=0)
        below = jnp.concatenate([block[half_lanes:] for block in turned], axis=0)
        result = jnp.dot(above, mixes[0], preferred_element_type=jnp.float32)
        result = result + jnp.dot(below, mixes[1], preferred_element_type=jnp.float32)
        for slot in range(group):
            both = result[half_lanes * slot : half_lanes * (slot + 1)]
            made[begin + slot] = both[:quarter].reshape(made.shape[1:])
            if high + begin + slot < slots:
                made[high + begin + slot] = both[quarter:].reshape(made.shape[1:])
        for first in (begin, high + begin):
            if first < slots:
                copy = pltpu.make_async_copy(
                    made.at[first : first + group], out_ref.at[first : first + group], sems.at[len(copies)]
                )
                copy.start()
                copies.append(copy)
    for copy in copies:
        copy.wait()


def middle_first(count):
    cores = 2
    side = math.isqrt(count // cores)
    half = side // 2
    return [
        ((i // (side * cores) + half) % side * side + (i // cores + half) % side) * cores + cores - 1 - i % cores
        for i in range(count)
    ]


def near(x):
    return pltpu.with_memory_space_constraint(x, pltpu.VMEM)


def far(x):
    return pltpu.with_memory_space_constraint(x, pltpu.HBM)


def exchange(blocks, order):
    count = lax.axis_size("lev")
    moved = {0: blocks[0]}
    for shift in order:
        moved[shift] = lax.ppermute(blocks[shift], "lev", [(i, (i + shift) % count) for i in range(count)])
    return moved


def body(adjoint_grid, lower_diffusion, upper_diffusion, row_lengths, wave_order):
    lev_count = lax.axis_size("lev")
    lat_count = lax.axis_size("lat")
    levels, rows, fields, points = adjoint_grid.shape
    waves = wave_order.shape[0]
    _, _, window = sizes(points, lev_count)
    f32, bf16 = jnp.float32, jnp.bfloat16
    members = levels * fields
    order = sorted(range(lev_count), key=lambda shift: min(shift, lev_count - shift))
    farthest_first = sorted(order[1:], key=lambda shift: -min(shift, lev_count - shift))
    windows = pltpu.VMEM((rows, members, window), bf16)
    made = pl.pallas_call(
        lambda *refs: pack_kernel(lev_count, order, *refs),
        out_shape=[pltpu.VMEM((rows * members, window), bf16)] * lev_count
        + [pltpu.VMEM((rows, LANE), jnp.int32)],
        in_specs=[ANY] * 2,
        out_specs=[VMEM] * (lev_count + 1),
        scratch_shapes=[
            pltpu.VMEM(adjoint_grid.shape, bf16),
            pltpu.SMEM(row_lengths.shape, jnp.int32),
            pltpu.SemaphoreType.DMA((levels + 1,)),
        ],
        name="pack",
        compiler_params=LIMIT,
    )(far(adjoint_grid), far(row_lengths))
    packed = dict(zip(order, made))
    limit = made[-1]
    arrived = exchange(packed, order[1:])
    factor = pltpu.VMEM((lev_count, rows * members, window), f32)
    factors = pl.pallas_call(
        lambda *refs: factor_kernel(lev_count, points, fields, *refs),
        out_shape=[factor] * 3,
        in_specs=[ANY] * 3,
        out_specs=[VMEM] * 3,
        scratch_shapes=[
            pltpu.VMEM(lower_diffusion.shape, f32),
            pltpu.VMEM(upper_diffusion.shape, f32),
            pltpu.SemaphoreType.DMA((2,)),
        ],
        name="factor",
        compiler_params=LIMIT,
        cost_estimate=pl.CostEstimate(flops=10_000_000, bytes_accessed=4_000_000, transcendentals=0),
    )(far(lower_diffusion), far(upper_diffusion), packed[0])
    solved = pl.pallas_call(
        lambda *refs: solve_kernel(lev_count, points, fields, *refs),
        out_shape=[windows] * lev_count,
        in_specs=[VMEM] * (4 + lev_count),
        out_specs=[VMEM] * lev_count,
        scratch_shapes=[
            pltpu.VMEM((lev_count, rows * members, window), f32),
            pltpu.VMEM((lev_count, rows, members, window), f32),
        ],
        name="solve",
        compiler_params=LIMIT,
    )(near(limit), *[near(x) for x in factors], *[near(arrived[shift]) for shift in range(lev_count)])
    returned = exchange(solved, farthest_first)
    fine, coarse = pl.pallas_call(
        table_kernel,
        out_shape=[pltpu.VMEM((rows, DEEP, 2 * waves), bf16), pltpu.VMEM((rows, 2, 24, waves), f32)],
        in_specs=[VMEM, VMEM, ANY],
        out_specs=[VMEM] * 2,
        name="table",
        compiler_params=LIMIT,
        cost_estimate=pl.CostEstimate(flops=10_000_000, bytes_accessed=4_000_000, transcendentals=0),
    )(near(limit), wave_order[None, :], solved[0])
    slots = waves // lat_count
    inner = 4
    high = slots // 2
    members_order = middle_first(lat_count)
    sums = pltpu.VMEM((rows, 2, waves // LANE, members, LANE), f32)
    begun = []
    for ready in ((0, farthest_first[0]), farthest_first[1:2]):
        begun = [
            pl.pallas_call(
                lambda *refs, ready=ready: early_kernel(lev_count, points, ready, *refs),
                out_shape=sums,
                in_specs=[VMEM] * (2 + len(ready) + len(begun)),
                out_specs=VMEM,
                name="early",
                cost_estimate=pl.CostEstimate(flops=500_000_000, bytes_accessed=4_000_000, transcendentals=0),
                compiler_params=LIMIT,
            )(near(fine), near(coarse), *[near(returned[shift]) for shift in ready], *[near(x) for x in begun])
        ]
    begun = begun[0]
    early = (0, *farthest_first[:2])
    sent = pl.pallas_call(
        lambda *refs: fourier_kernel(lev_count, points, early, members_order, *refs),
        out_shape=pltpu.VMEM((lat_count, high // inner, inner, LANE), bf16),
        in_specs=[VMEM] * (3 + lev_count),
        out_specs=VMEM,
        scratch_shapes=[sums, pltpu.VMEM((waves, LANE), f32)],
        name="fourier",
        compiler_params=LIMIT,
    )(near(fine), near(coarse), near(begun), *[near(returned[shift]) for shift in range(lev_count)])
    received = lax.all_to_all(
        sent, "lat", split_axis=0, concat_axis=0, tiled=True, axis_index_groups=[members_order]
    )
    return pl.pallas_call(
        lambda *refs: pair_kernel(members_order, *refs),
        out_shape=jax.ShapeDtypeStruct((slots, 2, fields, levels, rows * lat_count), f32),
        in_specs=[VMEM],
        out_specs=ANY,
        scratch_shapes=[
            pltpu.VMEM((lat_count * high, LANE), f32),
            pltpu.VMEM((slots, 2, fields, levels, rows * lat_count), f32),
            pltpu.SemaphoreType.DMA((slots // 4,)),
        ],
        name="pair",
        compiler_params=LIMIT,
    )(near(received))


def solution(mesh):
    in_specs = (P("lev", "lat", None, None), P(None, "lat", "lev"), P(None, "lat", "lev"), P(), P())
    out_specs = P("lat", None, None, "lev", None)
    return jax.shard_map(body, mesh=mesh, in_specs=in_specs, out_specs=out_specs, check_vma=False)
```
